32 devices in a mesh: aa: 4 (over y, x), ta: 8 (over z, core).
Axes of the slice: x: 2, y: 2, z: 4, core: 2. Of those that a mesh axis runs over, the one named last changes fastest.
Arguments:
- voltages: bfloat16 [1024, 49152], P('aa', 'ta'), may hold values from -6 to 6
Outputs:
- visibility: bfloat16 [2, 512, 1024, 1024], P(None, 'aa', 'ta')
The draws below stay inside these ranges and needn't reach their ends.
All inputs are finite; a program needn't handle non-finite values.
Results may differ from the reference program's by a relative error of at most 0.0078.
Values may be sent and summed in bfloat16 or wider, within the bound.
A program may use at most 256 MiB of HBM per device.

```python
import jax
import jax.numpy as jnp
from jax import lax

INPUTS = 1024
FRAME = 2048
CHANNELS = 512
TAPS = 4
SPECTRA = 24
SAMPLES = 49152


def level_of(stream_key, dims, pieces, smallest, high):
    gain = 1.0
    for axis_at, shards_of in pieces:
        draws = jax.random.uniform(jax.random.fold_in(jax.random.fold_in(stream_key, 6), axis_at), (shards_of,), jnp.float32, smallest / len(pieces), high / len(pieces))
        gain = gain * jnp.repeat(jnp.exp(draws), dims[axis_at] // shards_of).reshape((-1,) + (1,) * (len(dims) - 1 - axis_at))
    return gain


def noise(rng, dims, scale, reach, cuts=(), held_as=jnp.bfloat16):
    drawn = jax.random.normal(rng, dims, jnp.float32) * scale
    if len(cuts) > 0:
        drawn = level_of(rng, dims, cuts, -0.22, 0.18) * drawn
    return jnp.clip(drawn, min=-reach, max=reach).astype(held_as)


def setup_inputs(seed: int = 0) -> dict:
    arg_keys = jax.random.split(jax.random.key(seed), 2)
    voltages = noise(arg_keys[0], (INPUTS, SAMPLES), 1.0, 6.0, ((0, 4), (1, 8)))
    return {"voltages": voltages}


def make_window():
    length = TAPS * FRAME
    place = jnp.arange(length, dtype=jnp.float32)
    spread = (place - length / 2 + 0.5) / FRAME
    taper = 0.5 - 0.5 * jnp.cos(2.0 * jnp.pi * (place + 0.5) / length)
    return (jnp.sinc(spread) * taper).reshape(TAPS, FRAME)

def make_table():
    sample = jnp.arange(FRAME, dtype=jnp.int32)[:, None]
    channel = jnp.arange(CHANNELS, dtype=jnp.int32)[None, :]
    phase = (sample * channel % FRAME).astype(jnp.float32) * (2.0 * jnp.pi / FRAME)
    norm = 1.0 / jnp.sqrt(jnp.float32(FRAME))
    return (jnp.concatenate([jnp.cos(phase), -jnp.sin(phase)], axis=1) * norm).astype(jnp.bfloat16)

def correlate_one(block):
    real_part = block[0].astype(jnp.float32)
    imag_part = block[1].astype(jnp.float32)
    hi = lax.Precision.HIGHEST
    real_out = jnp.einsum('si,sj->ij', real_part, real_part, precision=hi) + jnp.einsum('si,sj->ij', imag_part, imag_part, precision=hi)
    imag_out = jnp.einsum('si,sj->ij', imag_part, real_part, precision=hi) - jnp.einsum('si,sj->ij', real_part, imag_part, precision=hi)
    return (jnp.stack([real_out, imag_out], axis=0) * (1.0 / SPECTRA)).astype(jnp.bfloat16)

def reference(voltages):
    window = make_window()
    table = make_table()
    frames = voltages.reshape(INPUTS, SPECTRA, FRAME).astype(jnp.float32)
    padded = jnp.concatenate([jnp.zeros((INPUTS, TAPS - 1, FRAME), jnp.float32), frames], axis=1)
    filtered = jnp.zeros((INPUTS, SPECTRA, FRAME), jnp.float32)
    for k in range(TAPS):
        filtered = filtered + window[k] * padded[:, k:k + SPECTRA, :]
    filtered = filtered.astype(jnp.bfloat16)
    spectra = jnp.dot(filtered.reshape(INPUTS * SPECTRA, FRAME), table, preferred_element_type=jnp.float32).astype(jnp.bfloat16)
    spectra = spectra.reshape(INPUTS, SPECTRA, 2, CHANNELS).transpose(3, 2, 1, 0)
    result = lax.map(correlate_one, spectra)
    return jnp.swapaxes(result, 0, 1)
```

```python
import functools

import jax
import jax.numpy as jnp
import ml_dtypes
import numpy as np
from jax import lax
from jax.experimental import pallas as pl
from jax.experimental.pallas import tpu as pltpu
from jax.sharding import PartitionSpec as P

INPUTS = 1024
FRAME = 2048
CHANNELS = 512
TAPS = 4
LANES = 128
COUNT = 3
QUADS = 32
ROWS = 24
PARTS = 4
STEP = QUADS // PARTS
GROUPS = 8
MESH = pl.DeviceIdType.MESH


def make_window():
    length = TAPS * FRAME
    place = np.arange(length, dtype=np.float64)
    spread = (place - length / 2 + 0.5) / FRAME
    taper = 0.5 - 0.5 * np.cos(2.0 * np.pi * (place + 0.5) / length)
    return (np.sinc(spread) * taper).reshape(TAPS, FRAME).astype(np.float32)


def make_table():
    part, target, quad, real, one = np.meshgrid(
        np.arange(PARTS), np.arange(4), np.arange(QUADS // PARTS), np.arange(2), np.arange(4), indexing="ij"
    )
    channel = (target * QUADS + part * (QUADS // PARTS) + quad) * 4 + one
    channel, real = channel.reshape(-1, 1), real.reshape(-1, 1)
    phase = (channel * np.arange(FRAME)[None, :] % FRAME) * (2.0 * np.pi / FRAME)
    values = np.where(real == 0, np.cos(phase), -np.sin(phase)) / np.sqrt(FRAME)
    return values.astype(ml_dtypes.bfloat16).reshape(PARTS, 2 * CHANNELS // PARTS, FRAME)


ORIGIN = (0, 0, 0, 1, 1, 2, 2, 3)


def units_of(group):
    if group % 2:
        return [((group // 2) * PARTS + j, j * STEP, STEP) for j in range(PARTS)]
    return [(4 * PARTS + group // 2, 0, QUADS)]


UNITS = 4 * PARTS + 4


def gather_kernel(
    voltages_ref,
    window_ref,
    table_hbm,
    out_ref,
    frames_ref,
    table_ref,
    filtered_ref,
    stage_ref,
    load_sem,
    swap_sem,
    halo_send,
    halo_recv,
    own_sem,
    aa_send,
    aa_recv,
    up_send,
    down_send,
    z_recv,
    core_send,
    core_recv,
):
    a, t = lax.axis_index("aa"), lax.axis_index("ta")
    z, core = t // 2, t % 2
    y, x = a // 2, a % 2
    other = 1 - core

    def at(chip, which, aa=None):
        return {"aa": a if aa is None else aa, "ta": chip * 2 + which}

    partners = [((y + k // 2) % 2) * 2 + (x + k % 2) % 2 for k in range(1, 4)]

    barrier = pltpu.get_barrier_semaphore()
    for k in range(3):
        pl.semaphore_signal(barrier, 1, device_id=at(z, core, partners[k]), device_id_type=MESH)
    pl.semaphore_signal(barrier, 1, device_id=at(z, other), device_id_type=MESH)
    for which in range(2):

        @pl.when(z > 0)
        def _():
            pl.semaphore_signal(barrier, 1, device_id=at(z - 1, which), device_id_type=MESH)

        @pl.when(z < 3)
        def _():
            pl.semaphore_signal(barrier, 1, device_id=at(z + 1, which), device_id_type=MESH)

    middle = jnp.where((z > 0) & (z < 3), 2, 0)
    pl.semaphore_wait(barrier, 6 + middle)

    table_copy = pltpu.make_async_copy(table_hbm, table_ref, load_sem.at[0])
    keep_copy = pltpu.make_async_copy(
        voltages_ref.at[pl.ds(core * LANES, LANES)], frames_ref.at[core], load_sem.at[1]
    )
    swap_copy = pltpu.make_async_remote_copy(
        src_ref=voltages_ref.at[pl.ds(other * LANES, LANES)],
        dst_ref=frames_ref.at[core],
        send_sem=swap_sem.at[0],
        recv_sem=swap_sem.at[1],
        device_id=at(z, other),
        device_id_type=MESH,
    )
    swap_in = pltpu.make_async_remote_copy(
        src_ref=voltages_ref.at[pl.ds(core * LANES, LANES)],
        dst_ref=frames_ref.at[other],
        send_sem=swap_sem.at[0],
        recv_sem=swap_sem.at[1],
        device_id=at(z, other),
        device_id_type=MESH,
    )

    def halo(which, chip):
        return pltpu.make_async_remote_copy(
            src_ref=voltages_ref.at[pl.ds(which * LANES, LANES)],
            dst_ref=frames_ref.at[2],
            send_sem=halo_send.at[which],
            recv_sem=halo_recv,
            device_id=at(chip, which),
            device_id_type=MESH,
        )

    swap_copy.start()
    keep_copy.start()
    table_copy.start()

    @pl.when((z > 0) & (core == 0))
    def _():
        for which in range(2):
            halo(which, z - 1).start()

    def form_filtered(current, earlier):
        def frame(start, place):
            if place < COUNT:
                block, column = earlier, place
            else:
                block, column = current, place - COUNT
            return frames_ref[
                block, pl.ds(start, 16), column * FRAME : (column + 1) * FRAME
            ].astype(jnp.float32)

        @pl.loop(0, LANES // 16)
        def _(step):
            start = pl.multiple_of(step * 16, 16)
            for s in range(COUNT):
                total = None
                for k in range(TAPS):
                    place = s + k + COUNT - TAPS + 1
                    if place < COUNT and earlier is None:
                        continue
                    term = window_ref[k : k + 1, :] * frame(start, place)
                    total = term if total is None else total + term
                filtered_ref[pl.ds(s * LANES + start, 16), :] = total.astype(jnp.bfloat16)

    def form_part(slot, j):
        product = lax.dot_general(
            table_ref[j],
            filtered_ref[...],
            (((1,), (1,)), ((), ())),
            preferred_element_type=jnp.float32,
        )
        pieces = [
            product[:, s * LANES : (s + 1) * LANES].reshape(4 * STEP, 8, LANES)
            for s in range(COUNT)
        ]
        block = jnp.concatenate(pieces, axis=1).astype(jnp.bfloat16)
        stage_ref[slot, :, pl.ds(j * STEP, STEP)] = block.reshape(4, STEP, ROWS, LANES)

    def to_owner(slot, group, number, quad, quads, k):
        return pltpu.make_async_remote_copy(
            src_ref=stage_ref.at[slot, partners[k], pl.ds(quad, quads)],
            dst_ref=out_ref.at[group, core, a, pl.ds(quad, quads)],
            send_sem=aa_send.at[number * 3 + k],
            recv_sem=aa_recv.at[number * 3 + k],
            device_id=at(z, core, partners[k]),
            device_id_type=MESH,
        )

    def from_source(slot, group, number, quad, quads, k):
        return pltpu.make_async_remote_copy(
            src_ref=stage_ref.at[slot, a, pl.ds(quad, quads)],
            dst_ref=out_ref.at[group, core, partners[k], pl.ds(quad, quads)],
            send_sem=aa_send.at[number * 3 + k],
            recv_sem=aa_recv.at[number * 3 + k],
            device_id=at(z, core, partners[k]),
            device_id_type=MESH,
        )

    def own(slot, group, number, quad, quads):
        return pltpu.make_async_copy(
            stage_ref.at[slot, a, pl.ds(quad, quads)],
            out_ref.at[group, core, a, pl.ds(quad, quads)],
            own_sem.at[number],
        )

    def exchange(slot, group, number, quad, quads):
        own(slot, group, number, quad, quads).start()
        for k in (2, 0, 1):
            to_owner(slot, group, number, quad, quads, k).start()

    def exchanged(slot, group, number, quad, quads):
        own(slot, group, number, quad, quads).wait()
        for k in range(3):
            from_source(slot, group, number, quad, quads, k).wait_recv()

    def exchange_sent(slot, group, number, quad, quads):
        for k in range(3):
            to_owner(slot, group, number, quad, quads, k).wait_send()

    def move(group, unit, quad, quads, which, send_sem, recv_sem, target):
        piece = out_ref.at[group, which, :, pl.ds(quad, quads)]
        return pltpu.make_async_remote_copy(
            src_ref=piece,
            dst_ref=piece,
            send_sem=send_sem.at[unit],
            recv_sem=recv_sem.at[unit],
            device_id=target,
            device_id_type=MESH,
        )

    def up(group, unit, quad, quads):
        return move(group, unit, quad, quads, core, up_send, z_recv, at(z + 1, core))

    def down(group, unit, quad, quads):
        return move(group, unit, quad, quads, core, down_send, z_recv, at(z - 1, core))

    def across(group, unit, quad, quads):
        return move(group, unit, quad, quads, core, core_send, core_recv, at(z, other))

    def from_core(group, unit, quad, quads):
        return move(group, unit, quad, quads, other, core_send, core_recv, at(z, other))

    def send_own(group, unit, quad, quads):
        pl.when(z < 3)(lambda: up(group, unit, quad, quads).start())
        pl.when(z > 0)(lambda: down(group, unit, quad, quads).start())
        across(group, unit, quad, quads).start()

    first = 2 * z + 1
    keep_copy.wait()
    swap_in.wait_recv()
    form_filtered(1, 0)
    table_copy.wait()

    def ready_first(j):
        exchanged(0, first, j, j * STEP, STEP)
        send_own(first, z * PARTS + j, j * STEP, STEP)

    @pl.loop(0, PARTS)
    def _(j):
        form_part(0, j)
        exchange(0, first, j, j * STEP, STEP)
        pl.when(j > 0)(lambda: ready_first(j - 1))

    @pl.when(z == 0)
    def _():
        form_filtered(0, None)
        ready_first(PARTS - 1)

        @pl.loop(0, PARTS)
        def _(j):
            form_part(2, j)

        exchange(2, 0, PARTS + 1, 0, QUADS)

    pl.when(z > 0)(lambda: ready_first(PARTS - 1))

    def take(chip, group):
        upward = ORIGIN[group] < chip
        for unit, quad, quads in units_of(group):
            if upward:
                down_like = up
            else:
                down_like = down
            down_like(group, unit, quad, quads).wait_recv()
            if upward and chip < 3:
                up(group, unit, quad, quads).start()
            if not upward and chip > 0:
                down(group, unit, quad, quads).start()
            across(group, unit, quad, quads).start()

    def in_order(chip, groups):
        @pl.when(z == chip)
        def _():
            for group in groups:
                take(chip, group)

    in_order(1, [1])
    in_order(2, [3])

    @pl.when(z == 0)
    def _():
        exchanged(2, 0, PARTS + 1, 0, QUADS)
        send_own(0, 4 * PARTS, 0, QUADS)

    second = 2 * z + 2

    @pl.when(z < 3)
    def _():
        halo(core, z).wait_recv()
        form_filtered(2, 1)

        @pl.loop(0, PARTS)
        def _(j):
            form_part(1, j)

        exchange(1, second, PARTS, 0, QUADS)

    in_order(1, [0])
    in_order(2, [1])

    @pl.when(z < 3)
    def _():
        exchanged(1, second, PARTS, 0, QUADS)
        send_own(second, 4 * PARTS + z + 1, 0, QUADS)

    in_order(0, [3, 5, 7, 4, 6])
    in_order(1, [5, 2, 7, 6])
    in_order(2, [7, 0, 4, 2])
    in_order(3, [5, 3, 1, 6, 0, 4, 2])

    swap_copy.wait_send()

    @pl.when((z > 0) & (core == 0))
    def _():
        for which in range(2):
            halo(which, z - 1).wait_send()

    @pl.loop(0, PARTS)
    def _(j):
        exchange_sent(0, first, j, j * STEP, STEP)

    pl.when(z == 0)(lambda: exchange_sent(2, 0, PARTS + 1, 0, QUADS))
    pl.when(z < 3)(lambda: exchange_sent(1, second, PARTS, 0, QUADS))
    for group in range(GROUPS):
        for unit, quad, quads in units_of(group):
            pl.when((z < 3) & (z >= ORIGIN[group]))(
                lambda: up(group, unit, quad, quads).wait_send()
            )
            pl.when((z > 0) & (z <= ORIGIN[group]))(
                lambda: down(group, unit, quad, quads).wait_send()
            )
            across(group, unit, quad, quads).wait_send()
            from_core(group, unit, quad, quads).wait_recv()


def gather(voltages, window, table):
    dma = pltpu.SemaphoreType.DMA
    return pl.pallas_call(
        gather_kernel,
        out_shape=jax.ShapeDtypeStruct((GROUPS, 2, 4, QUADS, ROWS, LANES), jnp.bfloat16),
        in_specs=[
            pl.BlockSpec(memory_space=pl.ANY),
            pl.BlockSpec(memory_space=pltpu.VMEM),
            pl.BlockSpec(memory_space=pl.ANY),
        ],
        out_specs=pl.BlockSpec(memory_space=pl.ANY),
        scratch_shapes=[
            pltpu.VMEM((3, LANES, COUNT * FRAME), jnp.bfloat16),
            pltpu.VMEM(table.shape, jnp.bfloat16),
            pltpu.VMEM((COUNT * LANES, FRAME), jnp.bfloat16),
            pltpu.VMEM((3, 4, QUADS, ROWS, LANES), jnp.bfloat16),
            dma((2,)),
            dma((2,)),
            dma((2,)),
            dma,
            dma((PARTS + 2,)),
            dma((3 * (PARTS + 2),)),
            dma((3 * (PARTS + 2),)),
            dma((UNITS,)),
            dma((UNITS,)),
            dma((UNITS,)),
            dma((UNITS,)),
            dma((UNITS,)),
        ],
        compiler_params=pltpu.CompilerParams(
            collective_id=0, has_side_effects=True, vmem_limit_bytes=40 * 2**20
        ),
        cost_estimate=pl.CostEstimate(
            flops=9 * 2**29, bytes_accessed=2**25, transcendentals=0
        ),
    )(voltages, window, table)


def correlate_kernel(where_ref, spectra_ref, spread_ref, out_ref, columns_ref, left_ref, *, scale):
    size = columns_ref.shape[0]
    full = GROUPS * ROWS
    columns_ref[full:, :] = jnp.zeros((size - full, INPUTS), jnp.bfloat16)
    rows = pl.ds(pl.multiple_of(where_ref[0] * LANES, LANES), LANES)
    channel_of = lax.broadcasted_iota(jnp.int32, (1, size), 1) % 4
    masks = [jnp.where(channel_of == c, 1.0, 0.0).astype(jnp.bfloat16) for c in range(4)]

    @pl.loop(0, spectra_ref.shape[3])
    def _(quad):
        for group in range(GROUPS):
            for aa in range(4):
                for core in range(2):
                    place = (aa * 2 + core) * LANES
                    columns_ref[group * ROWS : (group + 1) * ROWS, place : place + LANES] = (
                        spectra_ref[group, core, aa, quad]
                    )
        left = lax.dot_general(
            columns_ref[:, rows],
            spread_ref[...],
            (((0,), (0,)), ((), ())),
            preferred_element_type=jnp.float32,
        ).astype(jnp.bfloat16)
        for c in range(4):
            for p in range(2):
                place = (c * 2 + p) * LANES
                left_ref[place : place + LANES, :] = left[:, p * size : (p + 1) * size] * masks[c]
        for block in range(INPUTS // 256):
            here = slice(block * 256, (block + 1) * 256)
            total = jnp.dot(
                left_ref[...], columns_ref[:, here], preferred_element_type=jnp.float32
            )
            value = (total * scale).astype(jnp.bfloat16)
            for c in range(4):
                for p in range(2):
                    place = (c * 2 + p) * LANES
                    out_ref[p, quad * 4 + c, :, here] = value[place : place + LANES]


def make_spread():
    size = 256
    straight = np.zeros((size, size), np.float32)
    turned = np.zeros((size, size), np.float32)
    for row in range(GROUPS * ROWS):
        straight[row, row] = 1.0
        if row % 8 < 4:
            turned[row + 4, row] = 1.0
        else:
            turned[row - 4, row] = -1.0
    return np.concatenate([straight, turned], axis=1).astype(ml_dtypes.bfloat16)


def correlate(where, spectra, spread, scale):
    step = 2
    return pl.pallas_call(
        functools.partial(correlate_kernel, scale=scale),
        grid_spec=pltpu.PrefetchScalarGridSpec(
            num_scalar_prefetch=1,
            grid=(QUADS // step,),
            in_specs=[
                pl.BlockSpec(
                    (GROUPS, 2, 4, step, ROWS, LANES), lambda q, where_ref: (0, 0, 0, q, 0, 0)
                ),
                pl.BlockSpec(spread.shape, lambda q, where_ref: (0, 0)),
            ],
            out_specs=pl.BlockSpec(
                (2, 4 * step, LANES, INPUTS), lambda q, where_ref: (0, q, 0, 0)
            ),
            scratch_shapes=[
                pltpu.VMEM((256, INPUTS), jnp.bfloat16),
                pltpu.VMEM((8 * LANES, 256), jnp.bfloat16),
            ],
        ),
        out_shape=jax.ShapeDtypeStruct((2, 4 * QUADS, LANES, INPUTS), jnp.bfloat16),
        compiler_params=pltpu.CompilerParams(vmem_limit_bytes=50 * 2**20),
        cost_estimate=pl.CostEstimate(
            flops=2**34, bytes_accessed=80 * 2**20, transcendentals=0
        ),
    )(where, spectra, spread)


def shifted(value, axis, steps):
    count = lax.axis_size(axis)
    leading, last = (max(0, -steps), min(count, count - steps))
    return lax.ppermute(value, axis, [(source, source + steps) for source in range(leading, last)])


def plain_window():
    length = TAPS * FRAME
    place = jnp.arange(length, dtype=jnp.float32)
    spread = (place - length / 2 + 0.5) / FRAME
    taper = 0.5 - 0.5 * jnp.cos(2.0 * jnp.pi * (place + 0.5) / length)
    return (jnp.sinc(spread) * taper).reshape(TAPS, FRAME)


def plain_table():
    sample = jnp.arange(FRAME, dtype=jnp.int32)[:, None]
    column = jnp.arange(2 * CHANNELS, dtype=jnp.int32)[None, :]
    channel = column % CHANNELS
    phase = (sample * channel % FRAME).astype(jnp.float32) * (2.0 * jnp.pi / FRAME)
    norm = 1.0 / jnp.sqrt(jnp.float32(FRAME))
    values = jnp.where(column < CHANNELS, jnp.cos(phase), -jnp.sin(phase))
    return (values * norm).astype(jnp.bfloat16)


def left_operand(rows):
    first = jnp.concatenate([rows[0], rows[1]], axis=2)
    second = jnp.concatenate([rows[1], -rows[0]], axis=2)
    return jnp.stack([first, second], axis=0)


def plain_correlate(left, columns):
    return jnp.einsum("pcsi,pcsj->cij", left, columns, preferred_element_type=jnp.float32)


def finish(merged, row_count, scale):
    chan_dev = merged.shape[0]
    shaped = merged.reshape(chan_dev, 2, row_count, merged.shape[2])
    return (jnp.swapaxes(shaped, 0, 1) * scale).astype(jnp.bfloat16)


def plain_per_device(voltages):
    in_dev = voltages.shape[0]
    spec_dev = voltages.shape[1] // FRAME
    n_ta = lax.axis_size("ta")
    frames = voltages.reshape(in_dev, spec_dev, FRAME)
    earlier = shifted(frames, "ta", 1)
    padded = jnp.concatenate([earlier, frames], axis=1)
    window = plain_window()
    filtered = jnp.zeros((in_dev, spec_dev, FRAME), jnp.float32)
    for k in range(TAPS):
        filtered = filtered + window[k] * padded[:, k : k + spec_dev, :].astype(jnp.float32)
    filtered = filtered.astype(jnp.bfloat16)
    table = plain_table()
    spectra = jnp.einsum("isn,nk->ksi", filtered, table, preferred_element_type=jnp.float32).astype(
        jnp.bfloat16
    )
    spectra = spectra.reshape(2, CHANNELS, spec_dev, in_dev)
    row_count = INPUTS // n_ta
    scale = 1.0 / (spec_dev * n_ta)
    own_rows = lax.all_to_all(
        lax.all_to_all(spectra, "aa", split_axis=1, concat_axis=3, tiled=True),
        "ta",
        split_axis=3,
        concat_axis=2,
        tiled=True,
    )
    left = left_operand(own_rows)
    merged = plain_correlate(left, lax.all_gather(own_rows, "ta", axis=3, tiled=True))
    return finish(merged, row_count, scale)


def per_device(voltages):
    in_dev = voltages.shape[0]
    count = voltages.shape[1] // FRAME
    n_ta, n_aa = lax.axis_size("ta"), lax.axis_size("aa")
    fits = in_dev == 2 * LANES and n_ta == 8 and n_aa == 4 and count == COUNT
    if not fits or INPUTS != n_ta * LANES or CHANNELS != 4 * QUADS * n_aa:
        return plain_per_device(voltages)
    scale = 1.0 / (count * n_ta)
    spectra = gather(voltages, jnp.asarray(make_window()), jnp.asarray(make_table()))
    where = lax.axis_index("ta").astype(jnp.int32).reshape(1)
    return correlate(where, spectra, jnp.asarray(make_spread()), scale)


def solution(mesh):
    in_specs = (P("aa", "ta"),)
    out_specs = P(None, "aa", "ta", None)
    return jax.shard_map(
        per_device, mesh=mesh, in_specs=in_specs, out_specs=out_specs, check_vma=False
    )
```

```python
import functools

import jax
import jax.numpy as jnp
import ml_dtypes
import numpy as np
from jax import lax
from jax.experimental import pallas as pl
from jax.experimental.pallas import tpu as pltpu
from jax.sharding import PartitionSpec as P

INPUTS = 1024
FRAME = 2048
CHANNELS = 512
TAPS = 4
LANES = 128
COUNT = 3
QUADS = 32
ROWS = 24
PARTS = 4
STEP = QUADS // PARTS
GROUPS = 8
SWAP = 32
MESH = pl.DeviceIdType.MESH


def make_window():
    length = TAPS * FRAME
    place = np.arange(length, dtype=np.float64)
    spread = (place - length / 2 + 0.5) / FRAME
    taper = 0.5 - 0.5 * np.cos(2.0 * np.pi * (place + 0.5) / length)
    return (np.sinc(spread) * taper).reshape(TAPS, FRAME).astype(np.float32)


def make_table():
    part, target, quad, real, one = np.meshgrid(
        np.arange(PARTS), np.arange(4), np.arange(QUADS // PARTS), np.arange(2), np.arange(4), indexing="ij"
    )
    channel = (target * QUADS + part * (QUADS // PARTS) + quad) * 4 + one
    channel, real = channel.reshape(-1, 1), real.reshape(-1, 1)
    phase = (channel * np.arange(FRAME)[None, :] % FRAME) * (2.0 * np.pi / FRAME)
    values = np.where(real == 0, np.cos(phase), -np.sin(phase)) / np.sqrt(FRAME)
    return values.astype(ml_dtypes.bfloat16).reshape(PARTS, 2 * CHANNELS // PARTS, FRAME)


ORIGIN = (0, 0, 0, 1, 1, 2, 2, 3)


def units_of(group):
    if group % 2:
        return [((group // 2) * PARTS + j, j * STEP, STEP) for j in range(PARTS)]
    return [(4 * PARTS + group // 2, 0, QUADS)]


UNITS = 4 * PARTS + 4


def gather_kernel(
    voltages_ref,
    window_hbm,
    table_hbm,
    out_ref,
    frames_ref,
    window_ref,
    table_ref,
    filtered_ref,
    stage_ref,
    load_sem,
    swap_send,
    swap_recv,
    halo_send,
    halo_recv,
    own_sem,
    aa_send,
    aa_recv,
    up_send,
    down_send,
    z_recv,
    core_send,
    core_recv,
):
    a, t = lax.axis_index("aa"), lax.axis_index("ta")
    z, core = t // 2, t % 2
    y, x = a // 2, a % 2
    other = 1 - core

    def at(chip, which, aa=None):
        return {"aa": a if aa is None else aa, "ta": chip * 2 + which}

    partners = [((y + k // 2) % 2) * 2 + (x + k % 2) % 2 for k in range(1, 4)]

    barrier = pltpu.get_barrier_semaphore()
    for k in range(3):
        pl.semaphore_signal(barrier, 1, device_id=at(z, core, partners[k]), device_id_type=MESH)
    pl.semaphore_signal(barrier, 1, device_id=at(z, other), device_id_type=MESH)
    for which in range(2):

        @pl.when(z > 0)
        def _():
            pl.semaphore_signal(barrier, 1, device_id=at(z - 1, which), device_id_type=MESH)

        @pl.when(z < 3)
        def _():
            pl.semaphore_signal(barrier, 1, device_id=at(z + 1, which), device_id_type=MESH)

    middle = jnp.where((z > 0) & (z < 3), 2, 0)
    pl.semaphore_wait(barrier, 6 + middle)

    table_copy = pltpu.make_async_copy(table_hbm, table_ref, load_sem.at[0])
    keep_copy = pltpu.make_async_copy(
        voltages_ref.at[pl.ds(core * LANES, LANES)], frames_ref.at[core], load_sem.at[1]
    )
    window_copy = pltpu.make_async_copy(window_hbm, window_ref, load_sem.at[2])

    def swap_piece(piece, which, half):
        rows = pl.ds(pl.multiple_of(piece * SWAP, SWAP), SWAP)
        return pltpu.make_async_remote_copy(
            src_ref=voltages_ref.at[pl.ds(half * LANES + piece * SWAP, SWAP)],
            dst_ref=frames_ref.at[which, rows],
            send_sem=swap_send.at[piece],
            recv_sem=swap_recv.at[piece],
            device_id=at(z, other),
            device_id_type=MESH,
        )

    def swap_out(piece):
        return swap_piece(piece, core, other)

    def swap_in(piece):
        return swap_piece(piece, other, core)

    def halo(which, chip):
        return pltpu.make_async_remote_copy(
            src_ref=voltages_ref.at[pl.ds(which * LANES, LANES)],
            dst_ref=frames_ref.at[2],
            send_sem=halo_send.at[which],
            recv_sem=halo_recv,
            device_id=at(chip, which),
            device_id_type=MESH,
        )

    window_copy.start()
    keep_copy.start()
    for piece in range(LANES // SWAP):
        swap_out(piece).start()
    table_copy.start()

    @pl.when((z > 0) & (core == 0))
    def _():
        for which in range(2):
            halo(which, z - 1).start()

    def form_filtered(current, earlier, arrived=None):
        def frame(start, place):
            if place < COUNT:
                block, column = earlier, place
            else:
                block, column = current, place - COUNT
            return frames_ref[
                block, pl.ds(start, 16), column * FRAME : (column + 1) * FRAME
            ].astype(jnp.float32)

        @pl.loop(0, LANES // 16)
        def _(step):
            start = pl.multiple_of(step * 16, 16)
            if arrived is not None:
                every = SWAP // 16
                pl.when(step % every == 0)(lambda: arrived(step // every))
            for s in range(COUNT):
                total = None
                for k in range(TAPS):
                    place = s + k + COUNT - TAPS + 1
                    if place < COUNT and earlier is None:
                        continue
                    term = window_ref[k : k + 1, :] * frame(start, place)
                    total = term if total is None else total + term
                filtered_ref[pl.ds(s * LANES + start, 16), :] = total.astype(jnp.bfloat16)

    def form_part(slot, j):
        product = lax.dot_general(
            table_ref[j],
            filtered_ref[...],
            (((1,), (1,)), ((), ())),
            preferred_element_type=jnp.float32,
        )
        pieces = [
            product[:, s * LANES : (s + 1) * LANES].reshape(4 * STEP, 8, LANES)
            for s in range(COUNT)
        ]
        block = jnp.concatenate(pieces, axis=1).astype(jnp.bfloat16)
        stage_ref[slot, :, pl.ds(j * STEP, STEP)] = block.reshape(4, STEP, ROWS, LANES)

    def to_owner(slot, group, number, quad, quads, k):
        return pltpu.make_async_remote_copy(
            src_ref=stage_ref.at[slot, partners[k], pl.ds(quad, quads)],
            dst_ref=out_ref.at[group, core, a, pl.ds(quad, quads)],
            send_sem=aa_send.at[number * 3 + k],
            recv_sem=aa_recv.at[number * 3 + k],
            device_id=at(z, core, partners[k]),
            device_id_type=MESH,
        )

    def from_source(slot, group, number, quad, quads, k):
        return pltpu.make_async_remote_copy(
            src_ref=stage_ref.at[slot, a, pl.ds(quad, quads)],
            dst_ref=out_ref.at[group, core, partners[k], pl.ds(quad, quads)],
            send_sem=aa_send.at[number * 3 + k],
            recv_sem=aa_recv.at[number * 3 + k],
            device_id=at(z, core, partners[k]),
            device_id_type=MESH,
        )

    def own(slot, group, number, quad, quads):
        return pltpu.make_async_copy(
            stage_ref.at[slot, a, pl.ds(quad, quads)],
            out_ref.at[group, core, a, pl.ds(quad, quads)],
            own_sem.at[number],
        )

    def exchange(slot, group, number, quad, quads):
        own(slot, group, number, quad, quads).start()
        for k in (2, 0, 1):
            to_owner(slot, group, number, quad, quads, k).start()

    def exchanged(slot, group, number, quad, quads):
        own(slot, group, number, quad, quads).wait()
        for k in range(3):
            from_source(slot, group, number, quad, quads, k).wait_recv()

    def exchange_sent(slot, group, number, quad, quads):
        for k in range(3):
            to_owner(slot, group, number, quad, quads, k).wait_send()

    def move(group, unit, quad, quads, which, send_sem, recv_sem, target):
        piece = out_ref.at[group, which, :, pl.ds(quad, quads)]
        return pltpu.make_async_remote_copy(
            src_ref=piece,
            dst_ref=piece,
            send_sem=send_sem.at[unit],
            recv_sem=recv_sem.at[unit],
            device_id=target,
            device_id_type=MESH,
        )

    def up(group, unit, quad, quads):
        return move(group, unit, quad, quads, core, up_send, z_recv, at(z + 1, core))

    def down(group, unit, quad, quads):
        return move(group, unit, quad, quads, core, down_send, z_recv, at(z - 1, core))

    def across(group, unit, quad, quads):
        return move(group, unit, quad, quads, core, core_send, core_recv, at(z, other))

    def from_core(group, unit, quad, quads):
        return move(group, unit, quad, quads, other, core_send, core_recv, at(z, other))

    def send_own(group, unit, quad, quads):
        pl.when(z < 3)(lambda: up(group, unit, quad, quads).start())
        pl.when(z > 0)(lambda: down(group, unit, quad, quads).start())
        across(group, unit, quad, quads).start()

    first = 2 * z + 1
    window_copy.wait()
    keep_copy.wait()
    form_filtered(1, 0, lambda piece: swap_in(piece).wait_recv())
    table_copy.wait()

    def ready_first(j):
        exchanged(0, first, j, j * STEP, STEP)
        send_own(first, z * PARTS + j, j * STEP, STEP)

    @pl.loop(0, PARTS)
    def _(j):
        form_part(0, j)
        exchange(0, first, j, j * STEP, STEP)
        pl.when(j > 0)(lambda: ready_first(j - 1))

    @pl.when(z == 0)
    def _():
        form_filtered(0, None)
        ready_first(PARTS - 1)

        @pl.loop(0, PARTS)
        def _(j):
            form_part(2, j)

        exchange(2, 0, PARTS + 1, 0, QUADS)

    pl.when(z > 0)(lambda: ready_first(PARTS - 1))

    def take(chip, group):
        upward = ORIGIN[group] < chip
        for unit, quad, quads in units_of(group):
            if upward:
                down_like = up
            else:
                down_like = down
            down_like(group, unit, quad, quads).wait_recv()
            if upward and chip < 3:
                up(group, unit, quad, quads).start()
            if not upward and chip > 0:
                down(group, unit, quad, quads).start()
            across(group, unit, quad, quads).start()

    def in_order(chip, groups):
        @pl.when(z == chip)
        def _():
            for group in groups:
                take(chip, group)

    in_order(1, [1])
    in_order(2, [3])

    @pl.when(z == 0)
    def _():
        exchanged(2, 0, PARTS + 1, 0, QUADS)
        send_own(0, 4 * PARTS, 0, QUADS)

    second = 2 * z + 2

    @pl.when(z < 3)
    def _():
        halo(core, z).wait_recv()
        form_filtered(2, 1)

        @pl.loop(0, PARTS)
        def _(j):
            form_part(1, j)

        exchange(1, second, PARTS, 0, QUADS)

    in_order(1, [0])
    in_order(2, [1])

    @pl.when(z < 3)
    def _():
        exchanged(1, second, PARTS, 0, QUADS)
        send_own(second, 4 * PARTS + z + 1, 0, QUADS)

    in_order(0, [3, 5, 7, 4, 6])
    in_order(1, [5, 2, 7, 6])
    in_order(2, [7, 0, 4, 2])
    in_order(3, [5, 3, 1, 6, 0, 4, 2])

    for piece in range(LANES // SWAP):
        swap_out(piece).wait_send()

    @pl.when((z > 0) & (core == 0))
    def _():
        for which in range(2):
            halo(which, z - 1).wait_send()

    @pl.loop(0, PARTS)
    def _(j):
        exchange_sent(0, first, j, j * STEP, STEP)

    pl.when(z == 0)(lambda: exchange_sent(2, 0, PARTS + 1, 0, QUADS))
    pl.when(z < 3)(lambda: exchange_sent(1, second, PARTS, 0, QUADS))
    for group in range(GROUPS):
        for unit, quad, quads in units_of(group):
            pl.when((z < 3) & (z >= ORIGIN[group]))(
                lambda: up(group, unit, quad, quads).wait_send()
            )
            pl.when((z > 0) & (z <= ORIGIN[group]))(
                lambda: down(group, unit, quad, quads).wait_send()
            )
            across(group, unit, quad, quads).wait_send()
            from_core(group, unit, quad, quads).wait_recv()


def gather(voltages, window, table):
    dma = pltpu.SemaphoreType.DMA
    return pl.pallas_call(
        gather_kernel,
        out_shape=jax.ShapeDtypeStruct((GROUPS, 2, 4, QUADS, ROWS, LANES), jnp.bfloat16),
        in_specs=[
            pl.BlockSpec(memory_space=pltpu.HBM),
            pl.BlockSpec(memory_space=pltpu.HBM),
            pl.BlockSpec(memory_space=pltpu.HBM),
        ],
        out_specs=pl.BlockSpec(memory_space=pltpu.HBM),
        scratch_shapes=[
            pltpu.VMEM((3, LANES, COUNT * FRAME), jnp.bfloat16),
            pltpu.VMEM(window.shape, jnp.float32),
            pltpu.VMEM(table.shape, jnp.bfloat16),
            pltpu.VMEM((COUNT * LANES, FRAME), jnp.bfloat16),
            pltpu.VMEM((3, 4, QUADS, ROWS, LANES), jnp.bfloat16),
            dma((3,)),
            dma((LANES // SWAP,)),
            dma((LANES // SWAP,)),
            dma((2,)),
            dma,
            dma((PARTS + 2,)),
            dma((3 * (PARTS + 2),)),
            dma((3 * (PARTS + 2),)),
            dma((UNITS,)),
            dma((UNITS,)),
            dma((UNITS,)),
            dma((UNITS,)),
            dma((UNITS,)),
        ],
        compiler_params=pltpu.CompilerParams(
            collective_id=0, has_side_effects=True, vmem_limit_bytes=62 * 2**20
        ),
        cost_estimate=pl.CostEstimate(
            flops=9 * 2**29, bytes_accessed=2**25, transcendentals=0
        ),
    )(voltages, window, table)


def correlate_kernel(where_ref, spectra_ref, spread_ref, out_ref, columns_ref, left_ref, *, scale):
    deep, size = columns_ref.shape[:2]
    full = GROUPS * ROWS
    rows = pl.ds(pl.multiple_of(where_ref[0] * LANES, LANES), LANES)
    channel_of = lax.broadcasted_iota(jnp.int32, (1, size), 1) % 4
    masks = [jnp.where(channel_of == c, 1.0, 0.0).astype(jnp.bfloat16) for c in range(4)]
    columns_ref[:, full:, :] = jnp.zeros((deep, size - full, INPUTS), jnp.bfloat16)

    def prepare(slot, quad):
        for group in range(GROUPS):
            for aa in range(4):
                for core in range(2):
                    place = (aa * 2 + core) * LANES
                    columns_ref[
                        slot, group * ROWS : (group + 1) * ROWS, place : place + LANES
                    ] = spectra_ref[group, core, aa, quad]
        left = lax.dot_general(
            columns_ref[slot, :, rows],
            spread_ref[...],
            (((0,), (0,)), ((), ())),
            preferred_element_type=jnp.float32,
        ).astype(jnp.bfloat16)
        for c in range(4):
            for p in range(2):
                place = (c * 2 + p) * LANES
                left_ref[slot, place : place + LANES, :] = (
                    left[:, p * size : (p + 1) * size] * masks[c]
                )

    def multiply(slot, quad):
        for block in range(INPUTS // 256):
            here = slice(block * 256, (block + 1) * 256)
            total = jnp.dot(
                left_ref[slot], columns_ref[slot, :, here], preferred_element_type=jnp.float32
            )
            value = (total * scale).astype(jnp.bfloat16)
            for c in range(4):
                for p in range(2):
                    place = (c * 2 + p) * LANES
                    out_ref[p, quad * 4 + c, :, here] = value[place : place + LANES]

    @pl.loop(0, spectra_ref.shape[3] // deep)
    def _(step):
        for slot in range(deep):
            prepare(slot, step * deep + slot)
        for slot in range(deep):
            multiply(slot, step * deep + slot)


def make_spread():
    size = 256
    straight = np.zeros((size, size), np.float32)
    turned = np.zeros((size, size), np.float32)
    for row in range(GROUPS * ROWS):
        straight[row, row] = 1.0
        if row % 8 < 4:
            turned[row + 4, row] = 1.0
        else:
            turned[row - 4, row] = -1.0
    return np.concatenate([straight, turned], axis=1).astype(ml_dtypes.bfloat16)


def correlate(where, spectra, spread, scale):
    step = deep = 4
    return pl.pallas_call(
        functools.partial(correlate_kernel, scale=scale),
        grid_spec=pltpu.PrefetchScalarGridSpec(
            num_scalar_prefetch=1,
            grid=(QUADS // step,),
            in_specs=[
                pl.BlockSpec(
                    (GROUPS, 2, 4, step, ROWS, LANES), lambda q, where_ref: (0, 0, 0, q, 0, 0)
                ),
                pl.BlockSpec(spread.shape, lambda q, where_ref: (0, 0)),
            ],
            out_specs=pl.BlockSpec(
                (2, 4 * step, LANES, INPUTS), lambda q, where_ref: (0, q, 0, 0)
            ),
            scratch_shapes=[
                pltpu.VMEM((deep, 256, INPUTS), jnp.bfloat16),
                pltpu.VMEM((deep, 8 * LANES, 256), jnp.bfloat16),
            ],
        ),
        out_shape=jax.ShapeDtypeStruct((2, 4 * QUADS, LANES, INPUTS), jnp.bfloat16),
        compiler_params=pltpu.CompilerParams(vmem_limit_bytes=50 * 2**20),
        cost_estimate=pl.CostEstimate(
            flops=2**34, bytes_accessed=80 * 2**20, transcendentals=0
        ),
    )(where, spectra, spread)


def shifted(value, axis, steps):
    count = lax.axis_size(axis)
    leading, last = (max(0, -steps), min(count, count - steps))
    return lax.ppermute(value, axis, [(source, source + steps) for source in range(leading, last)])


def plain_window():
    length = TAPS * FRAME
    place = jnp.arange(length, dtype=jnp.float32)
    spread = (place - length / 2 + 0.5) / FRAME
    taper = 0.5 - 0.5 * jnp.cos(2.0 * jnp.pi * (place + 0.5) / length)
    return (jnp.sinc(spread) * taper).reshape(TAPS, FRAME)


def plain_table():
    sample = jnp.arange(FRAME, dtype=jnp.int32)[:, None]
    column = jnp.arange(2 * CHANNELS, dtype=jnp.int32)[None, :]
    channel = column % CHANNELS
    phase = (sample * channel % FRAME).astype(jnp.float32) * (2.0 * jnp.pi / FRAME)
    norm = 1.0 / jnp.sqrt(jnp.float32(FRAME))
    values = jnp.where(column < CHANNELS, jnp.cos(phase), -jnp.sin(phase))
    return (values * norm).astype(jnp.bfloat16)


def left_operand(rows):
    first = jnp.concatenate([rows[0], rows[1]], axis=2)
    second = jnp.concatenate([rows[1], -rows[0]], axis=2)
    return jnp.stack([first, second], axis=0)


def plain_correlate(left, columns):
    return jnp.einsum("pcsi,pcsj->cij", left, columns, preferred_element_type=jnp.float32)


def finish(merged, row_count, scale):
    chan_dev = merged.shape[0]
    shaped = merged.reshape(chan_dev, 2, row_count, merged.shape[2])
    return (jnp.swapaxes(shaped, 0, 1) * scale).astype(jnp.bfloat16)


def plain_per_device(voltages):
    in_dev = voltages.shape[0]
    spec_dev = voltages.shape[1] // FRAME
    n_ta = lax.axis_size("ta")
    frames = voltages.reshape(in_dev, spec_dev, FRAME)
    earlier = shifted(frames, "ta", 1)
    padded = jnp.concatenate([earlier, frames], axis=1)
    window = plain_window()
    filtered = jnp.zeros((in_dev, spec_dev, FRAME), jnp.float32)
    for k in range(TAPS):
        filtered = filtered + window[k] * padded[:, k : k + spec_dev, :].astype(jnp.float32)
    filtered = filtered.astype(jnp.bfloat16)
    table = plain_table()
    spectra = jnp.einsum("isn,nk->ksi", filtered, table, preferred_element_type=jnp.float32).astype(
        jnp.bfloat16
    )
    spectra = spectra.reshape(2, CHANNELS, spec_dev, in_dev)
    row_count = INPUTS // n_ta
    scale = 1.0 / (spec_dev * n_ta)
    own_rows = lax.all_to_all(
        lax.all_to_all(spectra, "aa", split_axis=1, concat_axis=3, tiled=True),
        "ta",
        split_axis=3,
        concat_axis=2,
        tiled=True,
    )
    left = left_operand(own_rows)
    merged = plain_correlate(left, lax.all_gather(own_rows, "ta", axis=3, tiled=True))
    return finish(merged, row_count, scale)


def per_device(voltages):
    in_dev = voltages.shape[0]
    count = voltages.shape[1] // FRAME
    n_ta, n_aa = lax.axis_size("ta"), lax.axis_size("aa")
    fits = in_dev == 2 * LANES and n_ta == 8 and n_aa == 4 and count == COUNT
    if not fits or INPUTS != n_ta * LANES or CHANNELS != 4 * QUADS * n_aa:
        return plain_per_device(voltages)
    scale = 1.0 / (count * n_ta)
    spectra = gather(voltages, jnp.asarray(make_window()), jnp.asarray(make_table()))
    where = lax.axis_index("ta").astype(jnp.int32).reshape(1)
    return correlate(where, spectra, jnp.asarray(make_spread()), scale)


def solution(mesh):
    in_specs = (P("aa", "ta"),)
    out_specs = P(None, "aa", "ta", None)
    return jax.shard_map(
        per_device, mesh=mesh, in_specs=in_specs, out_specs=out_specs, check_vma=False
    )
```

```python
import functools

import jax
import jax.numpy as jnp
import ml_dtypes
import numpy as np
from jax import lax
from jax.experimental import pallas as pl
from jax.experimental.pallas import tpu as pltpu
from jax.sharding import PartitionSpec as P

INPUTS = 1024
FRAME = 2048
CHANNELS = 512
TAPS = 4
LANES = 128
COUNT = 3
QUADS = 32
ROWS = 24
PARTS = 4
STEP = QUADS // PARTS
GROUPS = 8
SWAP = 32
KEPT = QUADS - STEP
HALF = STEP // 2
MESH = pl.DeviceIdType.MESH


def make_window():
    length = TAPS * FRAME
    place = np.arange(length, dtype=np.float64)
    spread = (place - length / 2 + 0.5) / FRAME
    taper = 0.5 - 0.5 * np.cos(2.0 * np.pi * (place + 0.5) / length)
    return (np.sinc(spread) * taper).reshape(TAPS, FRAME).astype(np.float32)


def make_table():
    part, target, quad, real, one = np.meshgrid(
        np.arange(PARTS), np.arange(4), np.arange(QUADS // PARTS), np.arange(2), np.arange(4), indexing="ij"
    )
    channel = (target * QUADS + part * (QUADS // PARTS) + quad) * 4 + one
    channel, real = channel.reshape(-1, 1), real.reshape(-1, 1)
    phase = (channel * np.arange(FRAME)[None, :] % FRAME) * (2.0 * np.pi / FRAME)
    values = np.where(real == 0, np.cos(phase), -np.sin(phase)) / np.sqrt(FRAME)
    return values.astype(ml_dtypes.bfloat16).reshape(PARTS, 2 * CHANNELS // PARTS, FRAME)


ORIGIN = (0, 0, 0, 1, 1, 2, 2, 3)


def units_of(group):
    return [(group * PARTS + j, j * STEP, STEP) for j in range(PARTS)]


UNITS = GROUPS * PARTS

UP_LATE = (5, 6, 2, 4, 0)
DOWN_LATE = (3, 4, 6, 7, 5)
LATE = len(UP_LATE)


def late_up(group, quad):
    return isinstance(quad, int) and quad >= KEPT and group in UP_LATE


def late_down(group, quad):
    return isinstance(quad, int) and quad >= KEPT and group in DOWN_LATE


def gather_kernel(
    voltages_ref,
    window_hbm,
    table_hbm,
    out_ref,
    rest_ref,
    late_ref,
    frames_ref,
    window_ref,
    table_ref,
    filtered_ref,
    stage_ref,
    load_sem,
    swap_send,
    swap_recv,
    halo_send,
    halo_recv,
    own_sem,
    late_sem,
    aa_send,
    aa_recv,
    up_send,
    down_send,
    z_recv,
    core_send,
    core_recv,
):
    a, t = lax.axis_index("aa"), lax.axis_index("ta")
    z, core = t // 2, t % 2
    y, x = a // 2, a % 2
    other = 1 - core

    def at(chip, which, aa=None):
        return {"aa": a if aa is None else aa, "ta": chip * 2 + which}

    partners = [((y + k // 2) % 2) * 2 + (x + k % 2) % 2 for k in range(1, 4)]

    table_copy = pltpu.make_async_copy(table_hbm, table_ref, load_sem.at[0])
    keep_copy = pltpu.make_async_copy(
        voltages_ref.at[pl.ds(core * LANES, LANES)], frames_ref.at[core], load_sem.at[1]
    )
    window_copy = pltpu.make_async_copy(window_hbm, window_ref, load_sem.at[2])

    def swap_piece(piece, which, half):
        rows = pl.ds(pl.multiple_of(piece * SWAP, SWAP), SWAP)
        return pltpu.make_async_remote_copy(
            src_ref=voltages_ref.at[pl.ds(half * LANES + piece * SWAP, SWAP)],
            dst_ref=frames_ref.at[which, rows],
            send_sem=swap_send.at[piece],
            recv_sem=swap_recv.at[piece],
            device_id=at(z, other),
            device_id_type=MESH,
        )

    def swap_out(piece):
        return swap_piece(piece, core, other)

    def swap_in(piece):
        return swap_piece(piece, other, core)

    def halo(which, chip):
        return pltpu.make_async_remote_copy(
            src_ref=voltages_ref.at[pl.ds(which * LANES, LANES)],
            dst_ref=frames_ref.at[2],
            send_sem=halo_send.at[which],
            recv_sem=halo_recv,
            device_id=at(chip, which),
            device_id_type=MESH,
        )

    keep_copy.start()
    window_copy.start()
    table_copy.start()

    barrier = pltpu.get_barrier_semaphore()
    for k in range(3):
        pl.semaphore_signal(barrier, 1, device_id=at(z, core, partners[k]), device_id_type=MESH)
    pl.semaphore_signal(barrier, 1, device_id=at(z, other), device_id_type=MESH)
    for which in range(2):

        @pl.when(z > 0)
        def _():
            pl.semaphore_signal(barrier, 1, device_id=at(z - 1, which), device_id_type=MESH)

        @pl.when(z < 3)
        def _():
            pl.semaphore_signal(barrier, 1, device_id=at(z + 1, which), device_id_type=MESH)

    middle = jnp.where((z > 0) & (z < 3), 2, 0)
    pl.semaphore_wait(barrier, 6 + middle)

    for piece in range(LANES // SWAP):
        swap_out(piece).start()

    @pl.when((z > 0) & (core == 0))
    def _():
        for which in range(2):
            halo(which, z - 1).start()

    def form_filtered(current, earlier, arrived=None):
        def frame(start, place):
            if place < COUNT:
                block, column = earlier, place
            else:
                block, column = current, place - COUNT
            return frames_ref[
                block, pl.ds(start, 16), column * FRAME : (column + 1) * FRAME
            ].astype(jnp.float32)

        @pl.loop(0, LANES // 16)
        def _(step):
            start = pl.multiple_of(step * 16, 16)
            if arrived is not None:
                every = SWAP // 16
                pl.when(step % every == 0)(lambda: arrived(step // every))
            for s in range(COUNT):
                total = None
                for k in range(TAPS):
                    place = s + k + COUNT - TAPS + 1
                    if place < COUNT and earlier is None:
                        continue
                    term = window_ref[k : k + 1, :] * frame(start, place)
                    total = term if total is None else total + term
                filtered_ref[pl.ds(s * LANES + start, 16), :] = total.astype(jnp.bfloat16)

    def form_part(slot, j):
        product = lax.dot_general(
            table_ref[j],
            filtered_ref[...],
            (((1,), (1,)), ((), ())),
            preferred_element_type=jnp.float32,
        )
        pieces = [
            product[:, s * LANES : (s + 1) * LANES].reshape(4 * STEP, 8, LANES)
            for s in range(COUNT)
        ]
        block = jnp.concatenate(pieces, axis=1).astype(jnp.bfloat16)
        stage_ref[slot, :, pl.ds(j * STEP, STEP)] = block.reshape(4, STEP, ROWS, LANES)

    def place(group, which, quad, quads, aa=None):
        ref, start = out_ref, quad
        if isinstance(quad, int) and quad >= KEPT:
            ref, start = rest_ref, quad - KEPT
        if aa is None:
            return ref.at[group, which, :, pl.ds(start, quads)]
        return ref.at[group, which, aa, pl.ds(start, quads)]

    def to_owner(slot, group, number, quad, quads, k):
        return pltpu.make_async_remote_copy(
            src_ref=stage_ref.at[slot, partners[k], pl.ds(quad, quads)],
            dst_ref=place(group, core, quad, quads, a),
            send_sem=aa_send.at[number * 3 + k],
            recv_sem=aa_recv.at[number * 3 + k],
            device_id=at(z, core, partners[k]),
            device_id_type=MESH,
        )

    def from_source(slot, group, number, quad, quads, k):
        return pltpu.make_async_remote_copy(
            src_ref=stage_ref.at[slot, a, pl.ds(quad, quads)],
            dst_ref=place(group, core, quad, quads, partners[k]),
            send_sem=aa_send.at[number * 3 + k],
            recv_sem=aa_recv.at[number * 3 + k],
            device_id=at(z, core, partners[k]),
            device_id_type=MESH,
        )

    def own(slot, group, number, quad, quads):
        return pltpu.make_async_copy(
            stage_ref.at[slot, a, pl.ds(quad, quads)],
            place(group, core, quad, quads, a),
            own_sem.at[number],
        )

    def exchange(slot, group, number, quad, quads):
        own(slot, group, number, quad, quads).start()
        for k in (2, 0, 1):
            to_owner(slot, group, number, quad, quads, k).start()

    def exchanged(slot, group, number, quad, quads):
        own(slot, group, number, quad, quads).wait()
        for k in range(3):
            from_source(slot, group, number, quad, quads, k).wait_recv()

    def exchange_sent(slot, group, number, quad, quads):
        for k in range(3):
            to_owner(slot, group, number, quad, quads, k).wait_send()

    def move(group, unit, quad, quads, which, send_sem, recv_sem, target):
        piece = place(group, which, quad, quads)
        return pltpu.make_async_remote_copy(
            src_ref=piece,
            dst_ref=piece,
            send_sem=send_sem.at[unit],
            recv_sem=recv_sem.at[unit],
            device_id=target,
            device_id_type=MESH,
        )

    def up(group, unit, quad, quads):
        return move(group, unit, quad, quads, core, up_send, z_recv, at(z + 1, core))

    def down(group, unit, quad, quads):
        return move(group, unit, quad, quads, core, down_send, z_recv, at(z - 1, core))

    def across(group, unit, quad, quads):
        return move(group, unit, quad, quads, core, core_send, core_recv, at(z, other))

    def from_core(group, unit, quad, quads):
        return move(group, unit, quad, quads, other, core_send, core_recv, at(z, other))

    def keep_late(number, group):
        return pltpu.make_async_copy(
            rest_ref.at[group, :, :, pl.ds(core * HALF, HALF)],
            late_ref.at[number],
            late_sem.at[number],
        )

    def send_own(group, unit, quad, quads, late=False):
        pl.when(z < (2 if late else 3))(lambda: up(group, unit, quad, quads).start())
        pl.when(z > (1 if late else 0))(lambda: down(group, unit, quad, quads).start())
        across(group, unit, quad, quads).start()

    first = 2 * z + 1
    window_copy.wait()
    keep_copy.wait()
    form_filtered(1, 0, lambda piece: swap_in(piece).wait_recv())
    table_copy.wait()

    def along(j, quad, aa, late):
        def copy(send_sem, chip):
            piece = place(first, core, quad, STEP, aa)
            return pltpu.make_async_remote_copy(
                src_ref=stage_ref.at[0, a, pl.ds(quad, STEP)] if aa is a else piece,
                dst_ref=piece,
                send_sem=send_sem.at[first * PARTS + j],
                recv_sem=z_recv.at[first * PARTS + j],
                device_id=at(chip, core),
                device_id_type=MESH,
            )

        pl.when(z < (2 if late else 3))(lambda: copy(up_send, z + 1).start())
        pl.when(z > (1 if late else 0))(lambda: copy(down_send, z - 1).start())

    def ready_first(j, quad, late=False):
        for k in range(3):
            from_source(0, first, j, quad, STEP, k).wait_recv()
            along(j, quad, partners[k], late)
        own(0, first, j, quad, STEP).wait()
        across(first, first * PARTS + j, quad, STEP).start()

    @pl.loop(0, PARTS - 1)
    def _(j):
        form_part(0, j)
        exchange(0, first, j, j * STEP, STEP)
        along(j, j * STEP, a, False)
        pl.when(j > 0)(lambda: ready_first(j - 1, (j - 1) * STEP))

    last = PARTS - 1
    form_part(0, last)
    exchange(0, first, last, KEPT, STEP)
    along(last, KEPT, a, True)
    ready_first(last - 1, KEPT - STEP)

    def ready_last():
        ready_first(last, KEPT, True)

    def whole(action, slot, group, number):
        action(slot, group, number, 0, KEPT)
        action(slot, group, number + 1, KEPT, QUADS - KEPT)

    @pl.when(z == 0)
    def _():
        form_filtered(0, None)
        ready_last()

        @pl.loop(0, PARTS)
        def _(j):
            form_part(2, j)

        whole(exchange, 2, 0, PARTS + 2)

    pl.when(z > 0)(ready_last)

    def take(chip, group):
        upward = ORIGIN[group] < chip
        onward = up if upward else down
        late = late_up if upward else late_down
        end, before = (3, 2) if upward else (0, 1)
        for unit, quad, quads in units_of(group):
            left = late(group, quad)
            if left and chip == end:
                continue
            onward(group, unit, quad, quads).wait_recv()
            if chip != end and not (left and chip == before):
                onward(group, unit, quad, quads).start()
            across(group, unit, quad, quads).start()

    def leave(chip, group):
        number = (UP_LATE if chip == 2 else DOWN_LATE).index(group)
        unit, quad, quads = units_of(group)[-1]
        from_core(group, unit, quad, quads).wait_recv()
        keep_late(number, group).start()

    def in_order(chip, groups, leaving=()):
        @pl.when(z == chip)
        def _():
            for number, group in enumerate(groups):
                take(chip, group)
                for after, done in leaving:
                    if after == number:
                        leave(chip, done)

    in_order(1, [1])
    in_order(2, [3])

    @pl.when(z == 0)
    def _():
        whole(exchanged, 2, 0, PARTS + 2)
        for unit, quad, quads in units_of(0):
            send_own(0, unit, quad, quads)

    second = 2 * z + 2

    @pl.when(z < 3)
    def _():
        halo(core, z).wait_recv()
        form_filtered(2, 1)

        @pl.loop(0, PARTS)
        def _(j):
            form_part(1, j)

        whole(exchange, 1, second, PARTS)

    in_order(1, [0])
    in_order(2, [1])

    @pl.when(z < 3)
    def _():
        whole(exchanged, 1, second, PARTS)
        for j in range(PARTS):
            send_own(second, second * PARTS + j, j * STEP, STEP, late=j == PARTS - 1)

    in_order(0, [3, 5, 7, 4, 6])
    in_order(1, [5, 2, 7, 6], [(0, 3), (1, 4), (1, 5), (3, 7), (3, 6)])
    in_order(2, [7, 0, 4, 2], [(0, 5), (1, 6), (2, 0), (3, 4), (3, 2)])
    in_order(3, [5, 3, 1, 6, 0, 4, 2])

    for piece in range(LANES // SWAP):
        swap_out(piece).wait_send()

    @pl.when((z > 0) & (core == 0))
    def _():
        for which in range(2):
            halo(which, z - 1).wait_send()

    @pl.loop(0, PARTS - 1)
    def _(j):
        exchange_sent(0, first, j, j * STEP, STEP)

    exchange_sent(0, first, last, KEPT, STEP)
    pl.when(z == 0)(lambda: whole(exchange_sent, 2, 0, PARTS + 2))
    pl.when(z < 3)(lambda: whole(exchange_sent, 1, second, PARTS))
    for group in range(GROUPS):
        for unit, quad, quads in units_of(group):
            top = 2 if late_up(group, quad) else 3
            bottom = 1 if late_down(group, quad) else 0
            pl.when((z < top) & (z >= ORIGIN[group]))(
                lambda: up(group, unit, quad, quads).wait_send()
            )
            pl.when((z > bottom) & (z <= ORIGIN[group]))(
                lambda: down(group, unit, quad, quads).wait_send()
            )

            crossed = received = z >= 0
            if late_up(group, quad):
                crossed, received = z < 3, z < 2
            if late_down(group, quad):
                crossed, received = crossed & (z > 0), received & (z > 1)
            pl.when(crossed)(lambda: across(group, unit, quad, quads).wait_send())
            pl.when(received)(lambda: from_core(group, unit, quad, quads).wait_recv())

    for number in range(LATE):
        pl.when(z == 2)(lambda: keep_late(number, UP_LATE[number]).wait())
        pl.when(z == 1)(lambda: keep_late(number, DOWN_LATE[number]).wait())


def gather(voltages, window, table):
    dma = pltpu.SemaphoreType.DMA
    return pl.pallas_call(
        gather_kernel,
        out_shape=[
            jax.ShapeDtypeStruct((GROUPS, 2, 4, KEPT, ROWS, LANES), jnp.bfloat16),
            jax.ShapeDtypeStruct((GROUPS, 2, 4, QUADS - KEPT, ROWS, LANES), jnp.bfloat16),
            jax.ShapeDtypeStruct((LATE, 2, 4, HALF, ROWS, LANES), jnp.bfloat16),
        ],
        in_specs=[
            pl.BlockSpec(memory_space=pltpu.HBM),
            pl.BlockSpec(memory_space=pltpu.HBM),
            pl.BlockSpec(memory_space=pltpu.HBM),
        ],
        out_specs=[pl.BlockSpec(memory_space=pltpu.HBM)] * 3,
        scratch_shapes=[
            pltpu.VMEM((3, LANES, COUNT * FRAME), jnp.bfloat16),
            pltpu.VMEM(window.shape, jnp.float32),
            pltpu.VMEM(table.shape, jnp.bfloat16),
            pltpu.VMEM((COUNT * LANES, FRAME), jnp.bfloat16),
            pltpu.VMEM((3, 4, QUADS, ROWS, LANES), jnp.bfloat16),
            dma((3,)),
            dma((LANES // SWAP,)),
            dma((LANES // SWAP,)),
            dma((2,)),
            dma,
            dma((PARTS + 4,)),
            dma((LATE,)),
            dma((3 * (PARTS + 4),)),
            dma((3 * (PARTS + 4),)),
            dma((UNITS,)),
            dma((UNITS,)),
            dma((UNITS,)),
            dma((UNITS,)),
            dma((UNITS,)),
        ],
        compiler_params=pltpu.CompilerParams(
            collective_id=0, has_side_effects=True, vmem_limit_bytes=62 * 2**20
        ),
        cost_estimate=pl.CostEstimate(
            flops=9 * 2**29, bytes_accessed=2**25, transcendentals=0
        ),
    )(voltages, window, table)


def correlate_kernel(where_ref, spectra_ref, spread_ref, *refs, scale, late):
    out_ref, columns_ref, left_ref = refs[-3:]
    deep, size = columns_ref.shape[:2]
    full = GROUPS * ROWS
    ta = where_ref[0]
    rows = pl.ds(pl.multiple_of(ta * LANES, LANES), LANES)
    channel_of = lax.broadcasted_iota(jnp.int32, (1, size), 1) % 4
    masks = [jnp.where(channel_of == c, 1.0, 0.0).astype(jnp.bfloat16) for c in range(4)]
    columns_ref[:, full:, :] = jnp.zeros((deep, size - full, INPUTS), jnp.bfloat16)

    def prepare(slot, quad, others):
        for group in range(GROUPS):
            down = slice(group * ROWS, (group + 1) * ROWS)
            for aa in range(4):
                for which in range(2):
                    place = (aa * 2 + which) * LANES
                    if group in others:
                        value = refs[0][others.index(group), which, aa, quad]
                    else:
                        value = spectra_ref[group, which, aa, quad]
                    columns_ref[slot, down, place : place + LANES] = value
        left = lax.dot_general(
            columns_ref[slot, :, rows],
            spread_ref[...],
            (((0,), (0,)), ((), ())),
            preferred_element_type=jnp.float32,
        ).astype(jnp.bfloat16)
        for c in range(4):
            for p in range(2):
                place = (c * 2 + p) * LANES
                left_ref[slot, place : place + LANES, :] = (
                    left[:, p * size : (p + 1) * size] * masks[c]
                )

    def multiply(slot, quad):
        for block in range(INPUTS // 256):
            here = slice(block * 256, (block + 1) * 256)
            total = jnp.dot(
                left_ref[slot], columns_ref[slot, :, here], preferred_element_type=jnp.float32
            )
            value = (total * scale).astype(jnp.bfloat16)
            for c in range(4):
                for p in range(2):
                    place = (c * 2 + p) * LANES
                    out_ref[p, quad * 4 + c, :, here] = value[place : place + LANES]

    def run(others):
        @pl.loop(0, spectra_ref.shape[3] // deep)
        def _(step):
            for slot in range(deep):
                prepare(slot, step * deep + slot, others)
            for slot in range(deep):
                multiply(slot, step * deep + slot)

    if not late:
        run(())
    else:
        pl.when(ta >= 6)(lambda: run(UP_LATE))
        pl.when(ta < 2)(lambda: run(DOWN_LATE))
        pl.when((ta >= 2) & (ta < 6))(lambda: run(()))


def make_spread():
    size = 256
    straight = np.zeros((size, size), np.float32)
    turned = np.zeros((size, size), np.float32)
    for row in range(GROUPS * ROWS):
        straight[row, row] = 1.0
        if row % 8 < 4:
            turned[row + 4, row] = 1.0
        else:
            turned[row - 4, row] = -1.0
    return np.concatenate([straight, turned], axis=1).astype(ml_dtypes.bfloat16)


def correlate(where, spectra, spread, scale, deep, quads, first=0, late=None, result=None):
    start = first // deep
    extra = [] if late is None else [late, result]
    late_specs = [
        pl.BlockSpec(
            (LATE, 2, 4, deep, ROWS, LANES), lambda q, where_ref: (0, 0, 0, q, 0, 0)
        ),
        pl.BlockSpec(memory_space=pl.ANY),
    ]
    return pl.pallas_call(
        functools.partial(correlate_kernel, scale=scale, late=late is not None),
        grid_spec=pltpu.PrefetchScalarGridSpec(
            num_scalar_prefetch=1,
            grid=(quads // deep,),
            in_specs=[
                pl.BlockSpec(
                    (GROUPS, 2, 4, deep, ROWS, LANES),
                    lambda q, where_ref: (0, 0, 0, where_ref[1] + q, 0, 0),
                ),
                pl.BlockSpec(spread.shape, lambda q, where_ref: (0, 0)),
            ]
            + late_specs[: len(extra)],
            out_specs=pl.BlockSpec(
                (2, 4 * deep, LANES, INPUTS),
                lambda q, where_ref: (0, start + where_ref[1] + q, 0, 0),
            ),
            scratch_shapes=[
                pltpu.VMEM((deep, 256, INPUTS), jnp.bfloat16),
                pltpu.VMEM((deep, 8 * LANES, 256), jnp.bfloat16),
            ],
        ),
        out_shape=jax.ShapeDtypeStruct((2, 4 * QUADS, LANES, INPUTS), jnp.bfloat16),
        input_output_aliases={4: 0} if extra else {},
        compiler_params=pltpu.CompilerParams(vmem_limit_bytes=50 * 2**20),
        cost_estimate=pl.CostEstimate(
            flops=quads * 2**29, bytes_accessed=quads * 5 * 2**19, transcendentals=0
        ),
    )(where, spectra, spread, *extra)


def shifted(value, axis, steps):
    count = lax.axis_size(axis)
    leading, last = (max(0, -steps), min(count, count - steps))
    return lax.ppermute(value, axis, [(source, source + steps) for source in range(leading, last)])


def plain_window():
    length = TAPS * FRAME
    place = jnp.arange(length, dtype=jnp.float32)
    spread = (place - length / 2 + 0.5) / FRAME
    taper = 0.5 - 0.5 * jnp.cos(2.0 * jnp.pi * (place + 0.5) / length)
    return (jnp.sinc(spread) * taper).reshape(TAPS, FRAME)


def plain_table():
    sample = jnp.arange(FRAME, dtype=jnp.int32)[:, None]
    column = jnp.arange(2 * CHANNELS, dtype=jnp.int32)[None, :]
    channel = column % CHANNELS
    phase = (sample * channel % FRAME).astype(jnp.float32) * (2.0 * jnp.pi / FRAME)
    norm = 1.0 / jnp.sqrt(jnp.float32(FRAME))
    values = jnp.where(column < CHANNELS, jnp.cos(phase), -jnp.sin(phase))
    return (values * norm).astype(jnp.bfloat16)


def left_operand(rows):
    first = jnp.concatenate([rows[0], rows[1]], axis=2)
    second = jnp.concatenate([rows[1], -rows[0]], axis=2)
    return jnp.stack([first, second], axis=0)


def plain_correlate(left, columns):
    return jnp.einsum("pcsi,pcsj->cij", left, columns, preferred_element_type=jnp.float32)


def finish(merged, row_count, scale):
    chan_dev = merged.shape[0]
    shaped = merged.reshape(chan_dev, 2, row_count, merged.shape[2])
    return (jnp.swapaxes(shaped, 0, 1) * scale).astype(jnp.bfloat16)


def plain_per_device(voltages):
    in_dev = voltages.shape[0]
    spec_dev = voltages.shape[1] // FRAME
    n_ta = lax.axis_size("ta")
    frames = voltages.reshape(in_dev, spec_dev, FRAME)
    earlier = shifted(frames, "ta", 1)
    padded = jnp.concatenate([earlier, frames], axis=1)
    window = plain_window()
    filtered = jnp.zeros((in_dev, spec_dev, FRAME), jnp.float32)
    for k in range(TAPS):
        filtered = filtered + window[k] * padded[:, k : k + spec_dev, :].astype(jnp.float32)
    filtered = filtered.astype(jnp.bfloat16)
    table = plain_table()
    spectra = jnp.einsum("isn,nk->ksi", filtered, table, preferred_element_type=jnp.float32).astype(
        jnp.bfloat16
    )
    spectra = spectra.reshape(2, CHANNELS, spec_dev, in_dev)
    row_count = INPUTS // n_ta
    scale = 1.0 / (spec_dev * n_ta)
    own_rows = lax.all_to_all(
        lax.all_to_all(spectra, "aa", split_axis=1, concat_axis=3, tiled=True),
        "ta",
        split_axis=3,
        concat_axis=2,
        tiled=True,
    )
    left = left_operand(own_rows)
    merged = plain_correlate(left, lax.all_gather(own_rows, "ta", axis=3, tiled=True))
    return finish(merged, row_count, scale)


def per_device(voltages):
    in_dev = voltages.shape[0]
    count = voltages.shape[1] // FRAME
    n_ta, n_aa = lax.axis_size("ta"), lax.axis_size("aa")
    fits = in_dev == 2 * LANES and n_ta == 8 and n_aa == 4 and count == COUNT
    if not fits or INPUTS != n_ta * LANES or CHANNELS != 4 * QUADS * n_aa:
        return plain_per_device(voltages)
    scale = 1.0 / (count * n_ta)
    spectra, rest, leaving = gather(
        voltages, jnp.asarray(make_window()), jnp.asarray(make_table())
    )
    ends = [(4, 6), (5, 7), (2, 0), (3, 1)]
    cores = [(6, 7), (7, 6), (0, 1), (1, 0)]
    mine = lax.ppermute(leaving, "ta", ends)
    spread = jnp.asarray(make_spread())
    me = lax.axis_index("ta").astype(jnp.int32)
    core, deep = me % 2, 2
    result = correlate(jnp.stack([me, 0]), spectra, spread, scale, 4, KEPT)
    mine, result = lax.optimization_barrier((mine, result))
    others = lax.ppermute(mine, "ta", cores)
    for half, late in ((core, mine), (1 - core, others)):
        where = jnp.stack([me, half * (HALF // deep)])
        result = correlate(where, rest, spread, scale, deep, HALF, KEPT, late, result)
    return result


def solution(mesh):
    in_specs = (P("aa", "ta"),)
    out_specs = P(None, "aa", "ta", None)
    return jax.shard_map(
        per_device, mesh=mesh, in_specs=in_specs, out_specs=out_specs, check_vma=False
    )
```

```python
import functools

import jax
import jax.numpy as jnp
import ml_dtypes
import numpy as np
from jax import lax
from jax.experimental import pallas as pl
from jax.experimental.pallas import tpu as pltpu
from jax.sharding import PartitionSpec as P

INPUTS = 1024
FRAME = 2048
CHANNELS = 512
TAPS = 4
LANES = 128
COUNT = 3
QUADS = 32
ROWS = 24
PARTS = 4
STEP = QUADS // PARTS
GROUPS = 8
SWAP = 16
KEPT = QUADS - STEP
HALF = STEP // 2
MESH = pl.DeviceIdType.MESH


def make_window():
    length = TAPS * FRAME
    place = np.arange(length, dtype=np.float64)
    spread = (place - length / 2 + 0.5) / FRAME
    taper = 0.5 - 0.5 * np.cos(2.0 * np.pi * (place + 0.5) / length)
    return (np.sinc(spread) * taper).reshape(TAPS, FRAME).astype(np.float32)


def make_table():
    part, target, quad, real, one = np.meshgrid(
        np.arange(PARTS), np.arange(4), np.arange(QUADS // PARTS), np.arange(2), np.arange(4), indexing="ij"
    )
    channel = (target * QUADS + part * (QUADS // PARTS) + quad) * 4 + one
    channel, real = channel.reshape(-1, 1), real.reshape(-1, 1)
    phase = (channel * np.arange(FRAME)[None, :] % FRAME) * (2.0 * np.pi / FRAME)
    values = np.where(real == 0, np.cos(phase), -np.sin(phase)) / np.sqrt(FRAME)
    return values.astype(ml_dtypes.bfloat16).reshape(PARTS, 2 * CHANNELS // PARTS, FRAME)


ORIGIN = (0, 0, 0, 1, 1, 2, 2, 3)


def units_of(group):
    return [(group * PARTS + j, j * STEP, STEP) for j in range(PARTS)]


UNITS = GROUPS * PARTS

UP_LATE = (5, 6, 2, 4, 0)
DOWN_LATE = (3, 4, 6, 7, 5)
LATE = len(UP_LATE)


def late_up(group, quad):
    return isinstance(quad, int) and quad >= KEPT and group in UP_LATE


def late_down(group, quad):
    return isinstance(quad, int) and quad >= KEPT and group in DOWN_LATE


def gather_kernel(
    voltages_ref,
    window_hbm,
    table_hbm,
    out_ref,
    rest_ref,
    late_ref,
    frames_ref,
    window_ref,
    table_ref,
    filtered_ref,
    stage_ref,
    load_sem,
    swap_send,
    swap_recv,
    halo_send,
    halo_recv,
    own_sem,
    late_sem,
    aa_send,
    aa_recv,
    up_send,
    down_send,
    z_recv,
    core_send,
    core_recv,
):
    a, t = lax.axis_index("aa"), lax.axis_index("ta")
    z, core = t // 2, t % 2
    y, x = a // 2, a % 2
    other = 1 - core

    def at(chip, which, aa=None):
        return {"aa": a if aa is None else aa, "ta": chip * 2 + which}

    partners = [((y + k // 2) % 2) * 2 + (x + k % 2) % 2 for k in range(1, 4)]

    table_copy = pltpu.make_async_copy(table_hbm, table_ref, load_sem.at[0])
    keep_copy = pltpu.make_async_copy(
        voltages_ref.at[pl.ds(core * LANES, LANES)], frames_ref.at[core], load_sem.at[1]
    )
    window_copy = pltpu.make_async_copy(window_hbm, window_ref, load_sem.at[2])

    def swap_piece(piece, which, half):
        rows = pl.ds(pl.multiple_of(piece * SWAP, SWAP), SWAP)
        return pltpu.make_async_remote_copy(
            src_ref=voltages_ref.at[pl.ds(half * LANES + piece * SWAP, SWAP)],
            dst_ref=frames_ref.at[which, rows],
            send_sem=swap_send.at[piece],
            recv_sem=swap_recv.at[piece],
            device_id=at(z, other),
            device_id_type=MESH,
        )

    def swap_out(piece):
        return swap_piece(piece, core, other)

    def swap_in(piece):
        return swap_piece(piece, other, core)

    def halo(which, chip):
        return pltpu.make_async_remote_copy(
            src_ref=voltages_ref.at[pl.ds(which * LANES, LANES)],
            dst_ref=frames_ref.at[2],
            send_sem=halo_send.at[which],
            recv_sem=halo_recv,
            device_id=at(chip, which),
            device_id_type=MESH,
        )

    keep_copy.start()
    window_copy.start()
    table_copy.start()

    barrier = pltpu.get_barrier_semaphore()
    for k in range(3):
        pl.semaphore_signal(barrier, 1, device_id=at(z, core, partners[k]), device_id_type=MESH)
    pl.semaphore_signal(barrier, 1, device_id=at(z, other), device_id_type=MESH)
    for which in range(2):

        @pl.when(z > 0)
        def _():
            pl.semaphore_signal(barrier, 1, device_id=at(z - 1, which), device_id_type=MESH)

        @pl.when(z < 3)
        def _():
            pl.semaphore_signal(barrier, 1, device_id=at(z + 1, which), device_id_type=MESH)

    middle = jnp.where((z > 0) & (z < 3), 2, 0)
    pl.semaphore_wait(barrier, 6 + middle)

    for piece in range(LANES // SWAP):
        swap_out(piece).start()

    @pl.when((z > 0) & (core == 0))
    def _():
        for which in range(2):
            halo(which, z - 1).start()

    def form_filtered(current, earlier, arrived=None):
        def frame(start, place):
            if place < COUNT:
                block, column = earlier, place
            else:
                block, column = current, place - COUNT
            return frames_ref[
                block, pl.ds(start, 16), column * FRAME : (column + 1) * FRAME
            ].astype(jnp.float32)

        @pl.loop(0, LANES // 16)
        def _(step):
            start = pl.multiple_of(step * 16, 16)
            if arrived is not None:
                every = SWAP // 16
                pl.when(step % every == 0)(lambda: arrived(step // every))
            for s in range(COUNT):
                total = None
                for k in range(TAPS):
                    place = s + k + COUNT - TAPS + 1
                    if place < COUNT and earlier is None:
                        continue
                    term = window_ref[k : k + 1, :] * frame(start, place)
                    total = term if total is None else total + term
                filtered_ref[pl.ds(s * LANES + start, 16), :] = total.astype(jnp.bfloat16)

    def form_part(slot, j):
        product = lax.dot_general(
            table_ref[j],
            filtered_ref[...],
            (((1,), (1,)), ((), ())),
            preferred_element_type=jnp.float32,
        )
        pieces = [
            product[:, s * LANES : (s + 1) * LANES].reshape(4 * STEP, 8, LANES)
            for s in range(COUNT)
        ]
        block = jnp.concatenate(pieces, axis=1).astype(jnp.bfloat16)
        stage_ref[slot, :, pl.ds(j * STEP, STEP)] = block.reshape(4, STEP, ROWS, LANES)

    def place(group, which, quad, quads, aa=None):
        ref, start = out_ref, quad
        if isinstance(quad, int) and quad >= KEPT:
            ref, start = rest_ref, quad - KEPT
        if aa is None:
            return ref.at[group, which, :, pl.ds(start, quads)]
        return ref.at[group, which, aa, pl.ds(start, quads)]

    def to_owner(slot, group, number, quad, quads, k):
        return pltpu.make_async_remote_copy(
            src_ref=stage_ref.at[slot, partners[k], pl.ds(quad, quads)],
            dst_ref=place(group, core, quad, quads, a),
            send_sem=aa_send.at[number * 3 + k],
            recv_sem=aa_recv.at[number * 3 + k],
            device_id=at(z, core, partners[k]),
            device_id_type=MESH,
        )

    def from_source(slot, group, number, quad, quads, k):
        return pltpu.make_async_remote_copy(
            src_ref=stage_ref.at[slot, a, pl.ds(quad, quads)],
            dst_ref=place(group, core, quad, quads, partners[k]),
            send_sem=aa_send.at[number * 3 + k],
            recv_sem=aa_recv.at[number * 3 + k],
            device_id=at(z, core, partners[k]),
            device_id_type=MESH,
        )

    def own(slot, group, number, quad, quads):
        return pltpu.make_async_copy(
            stage_ref.at[slot, a, pl.ds(quad, quads)],
            place(group, core, quad, quads, a),
            own_sem.at[number],
        )

    def exchange(slot, group, number, quad, quads):
        own(slot, group, number, quad, quads).start()
        for k in (2, 0, 1):
            to_owner(slot, group, number, quad, quads, k).start()

    def exchanged(slot, group, number, quad, quads):
        own(slot, group, number, quad, quads).wait()
        for k in range(3):
            from_source(slot, group, number, quad, quads, k).wait_recv()

    def exchange_sent(slot, group, number, quad, quads):
        for k in range(3):
            to_owner(slot, group, number, quad, quads, k).wait_send()

    def move(group, unit, quad, quads, which, send_sem, recv_sem, target):
        piece = place(group, which, quad, quads)
        return pltpu.make_async_remote_copy(
            src_ref=piece,
            dst_ref=piece,
            send_sem=send_sem.at[unit],
            recv_sem=recv_sem.at[unit],
            device_id=target,
            device_id_type=MESH,
        )

    def up(group, unit, quad, quads):
        return move(group, unit, quad, quads, core, up_send, z_recv, at(z + 1, core))

    def down(group, unit, quad, quads):
        return move(group, unit, quad, quads, core, down_send, z_recv, at(z - 1, core))

    def across(group, unit, quad, quads):
        return move(group, unit, quad, quads, core, core_send, core_recv, at(z, other))

    def from_core(group, unit, quad, quads):
        return move(group, unit, quad, quads, other, core_send, core_recv, at(z, other))

    def keep_late(number, group):
        return pltpu.make_async_copy(
            rest_ref.at[group, :, :, pl.ds(core * HALF, HALF)],
            late_ref.at[number],
            late_sem.at[number],
        )

    def send_own(group, unit, quad, quads, late=False):
        pl.when(z < (2 if late else 3))(lambda: up(group, unit, quad, quads).start())
        pl.when(z > (1 if late else 0))(lambda: down(group, unit, quad, quads).start())
        across(group, unit, quad, quads).start()

    first = 2 * z + 1
    window_copy.wait()
    keep_copy.wait()
    form_filtered(1, 0, lambda piece: swap_in(piece).wait_recv())
    table_copy.wait()

    def along(j, quad, aa, late):
        def copy(send_sem, chip):
            piece = place(first, core, quad, STEP, aa)
            return pltpu.make_async_remote_copy(
                src_ref=stage_ref.at[0, a, pl.ds(quad, STEP)] if aa is a else piece,
                dst_ref=piece,
                send_sem=send_sem.at[first * PARTS + j],
                recv_sem=z_recv.at[first * PARTS + j],
                device_id=at(chip, core),
                device_id_type=MESH,
            )

        pl.when(z < (2 if late else 3))(lambda: copy(up_send, z + 1).start())
        pl.when(z > (1 if late else 0))(lambda: copy(down_send, z - 1).start())

    def ready_first(j, quad, late=False):
        for k in range(3):
            from_source(0, first, j, quad, STEP, k).wait_recv()
            along(j, quad, partners[k], late)
        own(0, first, j, quad, STEP).wait()
        across(first, first * PARTS + j, quad, STEP).start()

    @pl.loop(0, PARTS - 1)
    def _(j):
        form_part(0, j)
        along(j, j * STEP, a, False)
        exchange(0, first, j, j * STEP, STEP)
        pl.when(j > 0)(lambda: ready_first(j - 1, (j - 1) * STEP))

    last = PARTS - 1
    form_part(0, last)
    exchange(0, first, last, KEPT, STEP)
    along(last, KEPT, a, True)
    ready_first(last - 1, KEPT - STEP)

    def ready_last():
        ready_first(last, KEPT, True)

    def whole(action, slot, group, number):
        action(slot, group, number, 0, KEPT)
        action(slot, group, number + 1, KEPT, QUADS - KEPT)

    @pl.when(z == 0)
    def _():
        form_filtered(0, None)
        ready_last()

        @pl.loop(0, PARTS)
        def _(j):
            form_part(2, j)

        whole(exchange, 2, 0, PARTS + 2)

    pl.when(z > 0)(ready_last)

    def take(chip, group):
        upward = ORIGIN[group] < chip
        onward = up if upward else down
        late = late_up if upward else late_down
        end, before = (3, 2) if upward else (0, 1)
        for unit, quad, quads in units_of(group):
            left = late(group, quad)
            if left and chip == end:
                continue
            onward(group, unit, quad, quads).wait_recv()
            if chip != end and not (left and chip == before):
                onward(group, unit, quad, quads).start()
            across(group, unit, quad, quads).start()

    def leave(chip, group):
        number = (UP_LATE if chip == 2 else DOWN_LATE).index(group)
        unit, quad, quads = units_of(group)[-1]
        from_core(group, unit, quad, quads).wait_recv()
        keep_late(number, group).start()

    def in_order(chip, groups, leaving=()):
        @pl.when(z == chip)
        def _():
            for number, group in enumerate(groups):
                take(chip, group)
                for after, done in leaving:
                    if after == number:
                        leave(chip, done)

    in_order(1, [1])
    in_order(2, [3])

    @pl.when(z == 0)
    def _():
        whole(exchanged, 2, 0, PARTS + 2)
        for unit, quad, quads in units_of(0):
            send_own(0, unit, quad, quads)

    second = 2 * z + 2

    @pl.when(z < 3)
    def _():
        halo(core, z).wait_recv()
        form_filtered(2, 1)

        @pl.loop(0, PARTS)
        def _(j):
            form_part(1, j)

        whole(exchange, 1, second, PARTS)

    in_order(1, [0])
    in_order(2, [1])

    @pl.when(z < 3)
    def _():
        whole(exchanged, 1, second, PARTS)
        for j in range(PARTS):
            send_own(second, second * PARTS + j, j * STEP, STEP, late=j == PARTS - 1)

    in_order(0, [3, 4, 5, 6, 7])
    in_order(1, [5, 2, 6, 7], [(0, 3), (1, 4), (1, 5), (3, 6), (3, 7)])
    in_order(2, [7, 0, 4, 2], [(0, 5), (1, 6), (2, 0), (3, 4), (3, 2)])
    in_order(3, [5, 3, 1, 6, 0, 4, 2])

    for piece in range(LANES // SWAP):
        swap_out(piece).wait_send()

    @pl.when((z > 0) & (core == 0))
    def _():
        for which in range(2):
            halo(which, z - 1).wait_send()

    @pl.loop(0, PARTS - 1)
    def _(j):
        exchange_sent(0, first, j, j * STEP, STEP)

    exchange_sent(0, first, last, KEPT, STEP)
    pl.when(z == 0)(lambda: whole(exchange_sent, 2, 0, PARTS + 2))
    pl.when(z < 3)(lambda: whole(exchange_sent, 1, second, PARTS))
    for group in range(GROUPS):
        for unit, quad, quads in units_of(group):
            top = 2 if late_up(group, quad) else 3
            bottom = 1 if late_down(group, quad) else 0
            pl.when((z < top) & (z >= ORIGIN[group]))(
                lambda: up(group, unit, quad, quads).wait_send()
            )
            pl.when((z > bottom) & (z <= ORIGIN[group]))(
                lambda: down(group, unit, quad, quads).wait_send()
            )

            crossed = received = z >= 0
            if late_up(group, quad):
                crossed, received = z < 3, z < 2
            if late_down(group, quad):
                crossed, received = crossed & (z > 0), received & (z > 1)
            pl.when(crossed)(lambda: across(group, unit, quad, quads).wait_send())
            pl.when(received)(lambda: from_core(group, unit, quad, quads).wait_recv())

    for number in range(LATE):
        pl.when(z == 2)(lambda: keep_late(number, UP_LATE[number]).wait())
        pl.when(z == 1)(lambda: keep_late(number, DOWN_LATE[number]).wait())


def gather(voltages, window, table):
    dma = pltpu.SemaphoreType.DMA
    return pl.pallas_call(
        gather_kernel,
        out_shape=[
            jax.ShapeDtypeStruct((GROUPS, 2, 4, KEPT, ROWS, LANES), jnp.bfloat16),
            jax.ShapeDtypeStruct((GROUPS, 2, 4, QUADS - KEPT, ROWS, LANES), jnp.bfloat16),
            jax.ShapeDtypeStruct((LATE, 2, 4, HALF, ROWS, LANES), jnp.bfloat16),
        ],
        in_specs=[
            pl.BlockSpec(memory_space=pltpu.HBM),
            pl.BlockSpec(memory_space=pltpu.HBM),
            pl.BlockSpec(memory_space=pltpu.HBM),
        ],
        out_specs=[pl.BlockSpec(memory_space=pltpu.HBM)] * 3,
        scratch_shapes=[
            pltpu.VMEM((3, LANES, COUNT * FRAME), jnp.bfloat16),
            pltpu.VMEM(window.shape, jnp.float32),
            pltpu.VMEM(table.shape, jnp.bfloat16),
            pltpu.VMEM((COUNT * LANES, FRAME), jnp.bfloat16),
            pltpu.VMEM((3, 4, QUADS, ROWS, LANES), jnp.bfloat16),
            dma((3,)),
            dma((LANES // SWAP,)),
            dma((LANES // SWAP,)),
            dma((2,)),
            dma,
            dma((PARTS + 4,)),
            dma((LATE,)),
            dma((3 * (PARTS + 4),)),
            dma((3 * (PARTS + 4),)),
            dma((UNITS,)),
            dma((UNITS,)),
            dma((UNITS,)),
            dma((UNITS,)),
            dma((UNITS,)),
        ],
        compiler_params=pltpu.CompilerParams(
            collective_id=0, has_side_effects=True, vmem_limit_bytes=62 * 2**20
        ),
        cost_estimate=pl.CostEstimate(
            flops=9 * 2**29, bytes_accessed=2**25, transcendentals=0
        ),
    )(voltages, window, table)


def correlator(ta, spectra_ref, spread_ref, late_ref, columns_ref, left_ref, scale):
    deep, size = columns_ref.shape[:2]
    full = GROUPS * ROWS
    rows = pl.ds(pl.multiple_of(ta * LANES, LANES), LANES)
    channel_of = lax.broadcasted_iota(jnp.int32, (1, size), 1) % 4
    masks = [jnp.where(channel_of == c, 1.0, 0.0).astype(jnp.bfloat16) for c in range(4)]
    columns_ref[:, full:, :] = jnp.zeros((deep, size - full, INPUTS), jnp.bfloat16)

    def prepare(slot, quad, others):
        for group in range(GROUPS):
            down = slice(group * ROWS, (group + 1) * ROWS)
            for aa in range(4):
                for which in range(2):
                    place = (aa * 2 + which) * LANES
                    if group in others:
                        value = late_ref[others.index(group), which, aa, quad]
                    else:
                        value = spectra_ref[group, which, aa, quad]
                    columns_ref[slot, down, place : place + LANES] = value
        left = lax.dot_general(
            columns_ref[slot, :, rows],
            spread_ref[...],
            (((0,), (0,)), ((), ())),
            preferred_element_type=jnp.float32,
        ).astype(jnp.bfloat16)
        for c in range(4):
            for p in range(2):
                place = (c * 2 + p) * LANES
                left_ref[slot, place : place + LANES, :] = (
                    left[:, p * size : (p + 1) * size] * masks[c]
                )

    def multiply(slot, store):
        for block in range(INPUTS // 256):
            here = slice(block * 256, (block + 1) * 256)
            total = jnp.dot(
                left_ref[slot], columns_ref[slot, :, here], preferred_element_type=jnp.float32
            )
            value = (total * scale).astype(jnp.bfloat16)
            for c in range(4):
                for p in range(2):
                    place = (c * 2 + p) * LANES
                    store(p, c, here, value[place : place + LANES])

    return prepare, multiply


def correlate_kernel(where_ref, spectra_ref, spread_ref, out_ref, columns_ref, left_ref, *, scale):
    deep = columns_ref.shape[0]
    prepare, multiply = correlator(
        where_ref[0], spectra_ref, spread_ref, None, columns_ref, left_ref, scale
    )

    @pl.loop(0, spectra_ref.shape[3] // deep)
    def _(step):
        for slot in range(deep):
            prepare(slot, step * deep + slot, ())
        for slot in range(deep):

            def store(p, c, here, value):
                out_ref[p, (step * deep + slot) * 4 + c, :, here] = value

            multiply(slot, store)


def finish_kernel(
    where_ref,
    rest_ref,
    spread_ref,
    late_hbm,
    result_ref,
    out_ref,
    spectra_ref,
    late_ref,
    columns_ref,
    left_ref,
    value_ref,
    load_sem,
    store_sem,
    *,
    scale,
):
    ta, half = where_ref[0], where_ref[1]
    loads = [
        pltpu.make_async_copy(
            rest_ref.at[:, :, :, pl.ds(half * HALF, HALF)], spectra_ref, load_sem.at[0]
        ),
        pltpu.make_async_copy(late_hbm, late_ref, load_sem.at[1]),
    ]
    for load in loads:
        load.start()
    prepare, multiply = correlator(
        ta, spectra_ref, spread_ref, late_ref, columns_ref, left_ref, scale
    )
    for load in loads:
        load.wait()

    def leave(quad):
        channel = (KEPT + half * HALF + quad) * 4
        return pltpu.make_async_copy(
            value_ref.at[quad], out_ref.at[:, pl.ds(channel, 4)], store_sem.at[quad]
        )

    def run(others):
        prepare(0, 0, others)
        for quad in range(HALF):
            if quad + 1 < HALF:
                prepare(quad + 1, quad + 1, others)

            def store(p, c, here, value):
                value_ref[quad, p, c, :, here] = value

            multiply(quad, store)
            leave(quad).start()

    pl.when(ta >= 6)(lambda: run(UP_LATE))
    pl.when(ta < 2)(lambda: run(DOWN_LATE))
    pl.when((ta >= 2) & (ta < 6))(lambda: run(()))
    for quad in range(HALF):
        leave(quad).wait()


def make_spread():
    size = 256
    straight = np.zeros((size, size), np.float32)
    turned = np.zeros((size, size), np.float32)
    for row in range(GROUPS * ROWS):
        straight[row, row] = 1.0
        if row % 8 < 4:
            turned[row + 4, row] = 1.0
        else:
            turned[row - 4, row] = -1.0
    return np.concatenate([straight, turned], axis=1).astype(ml_dtypes.bfloat16)


def correlate(where, spectra, spread, scale):
    quads, deep = spectra.shape[3], 4
    return pl.pallas_call(
        functools.partial(correlate_kernel, scale=scale),
        grid_spec=pltpu.PrefetchScalarGridSpec(
            num_scalar_prefetch=1,
            grid=(quads // deep,),
            in_specs=[
                pl.BlockSpec(
                    (GROUPS, 2, 4, deep, ROWS, LANES), lambda q, where_ref: (0, 0, 0, q, 0, 0)
                ),
                pl.BlockSpec(spread.shape, lambda q, where_ref: (0, 0)),
            ],
            out_specs=pl.BlockSpec(
                (2, 4 * deep, LANES, INPUTS), lambda q, where_ref: (0, q, 0, 0)
            ),
            scratch_shapes=[
                pltpu.VMEM((deep, 256, INPUTS), jnp.bfloat16),
                pltpu.VMEM((deep, 8 * LANES, 256), jnp.bfloat16),
            ],
        ),
        out_shape=jax.ShapeDtypeStruct((2, 4 * QUADS, LANES, INPUTS), jnp.bfloat16),
        compiler_params=pltpu.CompilerParams(vmem_limit_bytes=50 * 2**20),
        cost_estimate=pl.CostEstimate(
            flops=quads * 2**29, bytes_accessed=quads * 5 * 2**19, transcendentals=0
        ),
    )(where, spectra, spread)


def finish_half(where, rest, spread, late, result, scale):
    anywhere = pl.BlockSpec(memory_space=pl.ANY)
    return pl.pallas_call(
        functools.partial(finish_kernel, scale=scale),
        grid_spec=pltpu.PrefetchScalarGridSpec(
            num_scalar_prefetch=1,
            grid=(1,),
            in_specs=[
                anywhere,
                pl.BlockSpec(spread.shape, lambda q, where_ref: (0, 0)),
                anywhere,
                anywhere,
            ],
            out_specs=anywhere,
            scratch_shapes=[
                pltpu.VMEM((GROUPS, 2, 4, HALF, ROWS, LANES), jnp.bfloat16),
                pltpu.VMEM((LATE, 2, 4, HALF, ROWS, LANES), jnp.bfloat16),
                pltpu.VMEM((HALF, 256, INPUTS), jnp.bfloat16),
                pltpu.VMEM((HALF, 8 * LANES, 256), jnp.bfloat16),
                pltpu.VMEM((HALF, 2, 4, LANES, INPUTS), jnp.bfloat16),
                pltpu.SemaphoreType.DMA((2,)),
                pltpu.SemaphoreType.DMA((HALF,)),
            ],
        ),
        out_shape=jax.ShapeDtypeStruct(result.shape, result.dtype),
        input_output_aliases={4: 0},
        compiler_params=pltpu.CompilerParams(vmem_limit_bytes=50 * 2**20),
        cost_estimate=pl.CostEstimate(
            flops=HALF * 2**29, bytes_accessed=HALF * 5 * 2**19, transcendentals=0
        ),
    )(where, rest, spread, late, result)


def shifted(value, axis, steps):
    count = lax.axis_size(axis)
    leading, last = (max(0, -steps), min(count, count - steps))
    return lax.ppermute(value, axis, [(source, source + steps) for source in range(leading, last)])


def plain_window():
    length = TAPS * FRAME
    place = jnp.arange(length, dtype=jnp.float32)
    spread = (place - length / 2 + 0.5) / FRAME
    taper = 0.5 - 0.5 * jnp.cos(2.0 * jnp.pi * (place + 0.5) / length)
    return (jnp.sinc(spread) * taper).reshape(TAPS, FRAME)


def plain_table():
    sample = jnp.arange(FRAME, dtype=jnp.int32)[:, None]
    column = jnp.arange(2 * CHANNELS, dtype=jnp.int32)[None, :]
    channel = column % CHANNELS
    phase = (sample * channel % FRAME).astype(jnp.float32) * (2.0 * jnp.pi / FRAME)
    norm = 1.0 / jnp.sqrt(jnp.float32(FRAME))
    values = jnp.where(column < CHANNELS, jnp.cos(phase), -jnp.sin(phase))
    return (values * norm).astype(jnp.bfloat16)


def left_operand(rows):
    first = jnp.concatenate([rows[0], rows[1]], axis=2)
    second = jnp.concatenate([rows[1], -rows[0]], axis=2)
    return jnp.stack([first, second], axis=0)


def plain_correlate(left, columns):
    return jnp.einsum("pcsi,pcsj->cij", left, columns, preferred_element_type=jnp.float32)


def finish(merged, row_count, scale):
    chan_dev = merged.shape[0]
    shaped = merged.reshape(chan_dev, 2, row_count, merged.shape[2])
    return (jnp.swapaxes(shaped, 0, 1) * scale).astype(jnp.bfloat16)


def plain_per_device(voltages):
    in_dev = voltages.shape[0]
    spec_dev = voltages.shape[1] // FRAME
    n_ta = lax.axis_size("ta")
    frames = voltages.reshape(in_dev, spec_dev, FRAME)
    earlier = shifted(frames, "ta", 1)
    padded = jnp.concatenate([earlier, frames], axis=1)
    window = plain_window()
    filtered = jnp.zeros((in_dev, spec_dev, FRAME), jnp.float32)
    for k in range(TAPS):
        filtered = filtered + window[k] * padded[:, k : k + spec_dev, :].astype(jnp.float32)
    filtered = filtered.astype(jnp.bfloat16)
    table = plain_table()
    spectra = jnp.einsum("isn,nk->ksi", filtered, table, preferred_element_type=jnp.float32).astype(
        jnp.bfloat16
    )
    spectra = spectra.reshape(2, CHANNELS, spec_dev, in_dev)
    row_count = INPUTS // n_ta
    scale = 1.0 / (spec_dev * n_ta)
    own_rows = lax.all_to_all(
        lax.all_to_all(spectra, "aa", split_axis=1, concat_axis=3, tiled=True),
        "ta",
        split_axis=3,
        concat_axis=2,
        tiled=True,
    )
    left = left_operand(own_rows)
    merged = plain_correlate(left, lax.all_gather(own_rows, "ta", axis=3, tiled=True))
    return finish(merged, row_count, scale)


def per_device(voltages):
    in_dev = voltages.shape[0]
    count = voltages.shape[1] // FRAME
    n_ta, n_aa = lax.axis_size("ta"), lax.axis_size("aa")
    fits = in_dev == 2 * LANES and n_ta == 8 and n_aa == 4 and count == COUNT
    if not fits or INPUTS != n_ta * LANES or CHANNELS != 4 * QUADS * n_aa:
        return plain_per_device(voltages)
    scale = 1.0 / (count * n_ta)
    spectra, rest, leaving = gather(
        voltages, jnp.asarray(make_window()), jnp.asarray(make_table())
    )
    ends = [(4, 6), (5, 7), (2, 0), (3, 1)]
    cores = [(6, 7), (7, 6), (0, 1), (1, 0)]
    mine = lax.ppermute(leaving, "ta", ends)
    spread = jnp.asarray(make_spread())
    me = lax.axis_index("ta").astype(jnp.int32)
    core = me % 2
    result = correlate(me.reshape(1), spectra, spread, scale)
    mine, result = lax.optimization_barrier((mine, result))
    others = lax.ppermute(mine, "ta", cores)
    for half, late in ((core, mine), (1 - core, others)):
        result = finish_half(jnp.stack([me, half]), rest, spread, late, result, scale)
    return result


def solution(mesh):
    in_specs = (P("aa", "ta"),)
    out_specs = P(None, "aa", "ta", None)
    return jax.shard_map(
        per_device, mesh=mesh, in_specs=in_specs, out_specs=out_specs, check_vma=False
    )
```

```python
import functools

import jax
import jax.numpy as jnp
import ml_dtypes
import numpy as np
from jax import lax
from jax.experimental import pallas as pl
from jax.experimental.pallas import tpu as pltpu
from jax.sharding import PartitionSpec as P

INPUTS = 1024
FRAME = 2048
CHANNELS = 512
TAPS = 4
LANES = 128
COUNT = 3
QUADS = 32
ROWS = 24
PARTS = 4
STEP = QUADS // PARTS
GROUPS = 8
SWAP = 16
WIDE = 256


KEPT = QUADS - STEP
HALF = STEP // 2
MESH = pl.DeviceIdType.MESH


def make_window():
    length = TAPS * FRAME
    place = np.arange(length, dtype=np.float64)
    spread = (place - length / 2 + 0.5) / FRAME
    taper = 0.5 - 0.5 * np.cos(2.0 * np.pi * (place + 0.5) / length)
    return (np.sinc(spread) * taper).reshape(TAPS, FRAME).astype(np.float32)


def make_table():
    part, target, quad, real, one = np.meshgrid(
        np.arange(PARTS), np.arange(4), np.arange(QUADS // PARTS), np.arange(2), np.arange(4), indexing="ij"
    )
    channel = (target * QUADS + part * (QUADS // PARTS) + quad) * 4 + one
    channel, real = channel.reshape(-1, 1), real.reshape(-1, 1)
    phase = (channel * np.arange(FRAME)[None, :] % FRAME) * (2.0 * np.pi / FRAME)
    values = np.where(real == 0, np.cos(phase), -np.sin(phase)) / np.sqrt(FRAME)
    return values.astype(ml_dtypes.bfloat16).reshape(PARTS, 2 * CHANNELS // PARTS, FRAME)


ORIGIN = (0, 0, 0, 1, 1, 2, 2, 3)


def units_of(group):
    return [(group * PARTS + j, j * STEP, STEP) for j in range(PARTS)]


UNITS = GROUPS * PARTS

UP_LATE = (5, 6, 2, 4, 0)
DOWN_LATE = (3, 4, 6, 7, 5)
LATE = len(UP_LATE)


def late_up(group, quad):
    return isinstance(quad, int) and quad >= KEPT and group in UP_LATE


def late_down(group, quad):
    return isinstance(quad, int) and quad >= KEPT and group in DOWN_LATE


def gather_kernel(
    voltages_ref,
    window_hbm,
    table_hbm,
    out_ref,
    rest_ref,
    late_ref,
    frames_ref,
    window_ref,
    table_ref,
    filtered_ref,
    stage_ref,
    load_sem,
    swap_send,
    swap_recv,
    halo_send,
    halo_recv,
    own_sem,
    late_sem,
    aa_send,
    aa_recv,
    up_send,
    down_send,
    z_recv,
    core_send,
    core_recv,
):
    a, t = lax.axis_index("aa"), lax.axis_index("ta")
    z, core = t // 2, t % 2
    y, x = a // 2, a % 2
    other = 1 - core

    def at(chip, which, aa=None):
        return {"aa": a if aa is None else aa, "ta": chip * 2 + which}

    partners = [((y + k // 2) % 2) * 2 + (x + k % 2) % 2 for k in range(1, 4)]

    table_copy = pltpu.make_async_copy(table_hbm, table_ref, load_sem.at[0])
    keep_copy = pltpu.make_async_copy(
        voltages_ref.at[pl.ds(core * LANES, LANES)], frames_ref.at[core], load_sem.at[1]
    )
    window_copy = pltpu.make_async_copy(window_hbm, window_ref, load_sem.at[2])

    def swap_piece(piece, which, half):
        rows = pl.ds(pl.multiple_of(piece * SWAP, SWAP), SWAP)
        return pltpu.make_async_remote_copy(
            src_ref=voltages_ref.at[pl.ds(half * LANES + piece * SWAP, SWAP)],
            dst_ref=frames_ref.at[which, rows],
            send_sem=swap_send.at[piece],
            recv_sem=swap_recv.at[piece],
            device_id=at(z, other),
            device_id_type=MESH,
        )

    def swap_out(piece):
        return swap_piece(piece, core, other)

    def swap_in(piece):
        return swap_piece(piece, other, core)

    def halo(which, chip):
        return pltpu.make_async_remote_copy(
            src_ref=voltages_ref.at[pl.ds(which * LANES, LANES)],
            dst_ref=frames_ref.at[2],
            send_sem=halo_send.at[which],
            recv_sem=halo_recv,
            device_id=at(chip, which),
            device_id_type=MESH,
        )

    keep_copy.start()
    window_copy.start()
    table_copy.start()

    barrier = pltpu.get_barrier_semaphore()
    for k in range(3):
        pl.semaphore_signal(barrier, 1, device_id=at(z, core, partners[k]), device_id_type=MESH)
    pl.semaphore_signal(barrier, 1, device_id=at(z, other), device_id_type=MESH)
    for which in range(2):

        @pl.when(z > 0)
        def _():
            pl.semaphore_signal(barrier, 1, device_id=at(z - 1, which), device_id_type=MESH)

        @pl.when(z < 3)
        def _():
            pl.semaphore_signal(barrier, 1, device_id=at(z + 1, which), device_id_type=MESH)

    middle = jnp.where((z > 0) & (z < 3), 2, 0)
    pl.semaphore_wait(barrier, 6 + middle)

    for piece in range(LANES // SWAP):
        swap_out(piece).start()

    @pl.when((z > 0) & (core == 0))
    def _():
        for which in range(2):
            halo(which, z - 1).start()

    def form_filtered(current, earlier, arrived=None):
        first_place = 0 if earlier is not None else COUNT

        @pl.loop(0, LANES // 16)
        def _(step):
            start = pl.multiple_of(step * 16, 16)
            if arrived is not None:
                every = SWAP // 16
                pl.when(step % every == 0)(lambda: arrived(step // every))
            for column in range(0, FRAME, WIDE):
                frames = {}
                for place in range(first_place, 2 * COUNT):
                    block = earlier if place < COUNT else current
                    at_column = place % COUNT * FRAME + column
                    frames[place] = frames_ref[
                        block, pl.ds(start, 16), at_column : at_column + WIDE
                    ].astype(jnp.float32)
                taps = [window_ref[k : k + 1, column : column + WIDE] for k in range(TAPS)]
                for s in range(COUNT):
                    total = None
                    for k in range(TAPS):
                        place = s + k + COUNT - TAPS + 1
                        if place < first_place:
                            continue
                        term = taps[k] * frames[place]
                        total = term if total is None else total + term
                    filtered_ref[
                        pl.ds(s * LANES + start, 16), column : column + WIDE
                    ] = total.astype(jnp.bfloat16)

    def form_part(slot, j):
        product = lax.dot_general(
            table_ref[j],
            filtered_ref[...],
            (((1,), (1,)), ((), ())),
            preferred_element_type=jnp.float32,
        )
        pieces = [
            product[:, s * LANES : (s + 1) * LANES].reshape(4 * STEP, 8, LANES)
            for s in range(COUNT)
        ]
        block = jnp.concatenate(pieces, axis=1).astype(jnp.bfloat16)
        stage_ref[slot, :, pl.ds(j * STEP, STEP)] = block.reshape(4, STEP, ROWS, LANES)

    def place(group, which, quad, quads, aa=None):
        ref, start = out_ref, quad
        if isinstance(quad, int) and quad >= KEPT:
            ref, start = rest_ref, quad - KEPT
        if aa is None:
            return ref.at[group, which, :, pl.ds(start, quads)]
        return ref.at[group, which, aa, pl.ds(start, quads)]

    def to_owner(slot, group, number, quad, quads, k):
        return pltpu.make_async_remote_copy(
            src_ref=stage_ref.at[slot, partners[k], pl.ds(quad, quads)],
            dst_ref=place(group, core, quad, quads, a),
            send_sem=aa_send.at[number * 3 + k],
            recv_sem=aa_recv.at[number * 3 + k],
            device_id=at(z, core, partners[k]),
            device_id_type=MESH,
        )

    def from_source(slot, group, number, quad, quads, k):
        return pltpu.make_async_remote_copy(
            src_ref=stage_ref.at[slot, a, pl.ds(quad, quads)],
            dst_ref=place(group, core, quad, quads, partners[k]),
            send_sem=aa_send.at[number * 3 + k],
            recv_sem=aa_recv.at[number * 3 + k],
            device_id=at(z, core, partners[k]),
            device_id_type=MESH,
        )

    def own(slot, group, number, quad, quads):
        return pltpu.make_async_copy(
            stage_ref.at[slot, a, pl.ds(quad, quads)],
            place(group, core, quad, quads, a),
            own_sem.at[number],
        )

    def exchange(slot, group, number, quad, quads):
        own(slot, group, number, quad, quads).start()
        for k in (2, 0, 1):
            to_owner(slot, group, number, quad, quads, k).start()

    def exchanged(slot, group, number, quad, quads):
        own(slot, group, number, quad, quads).wait()
        for k in range(3):
            from_source(slot, group, number, quad, quads, k).wait_recv()

    def exchange_sent(slot, group, number, quad, quads):
        for k in range(3):
            to_owner(slot, group, number, quad, quads, k).wait_send()

    def move(group, unit, quad, quads, which, send_sem, recv_sem, target):
        piece = place(group, which, quad, quads)
        return pltpu.make_async_remote_copy(
            src_ref=piece,
            dst_ref=piece,
            send_sem=send_sem.at[unit],
            recv_sem=recv_sem.at[unit],
            device_id=target,
            device_id_type=MESH,
        )

    def up(group, unit, quad, quads):
        return move(group, unit, quad, quads, core, up_send, z_recv, at(z + 1, core))

    def down(group, unit, quad, quads):
        return move(group, unit, quad, quads, core, down_send, z_recv, at(z - 1, core))

    def across(group, unit, quad, quads):
        return move(group, unit, quad, quads, core, core_send, core_recv, at(z, other))

    def from_core(group, unit, quad, quads):
        return move(group, unit, quad, quads, other, core_send, core_recv, at(z, other))

    def keep_late(number, group):
        return pltpu.make_async_copy(
            rest_ref.at[group, :, :, pl.ds(core * HALF, HALF)],
            late_ref.at[number],
            late_sem.at[number],
        )

    def send_own(group, unit, quad, quads, late=False):
        pl.when(z < (2 if late else 3))(lambda: up(group, unit, quad, quads).start())
        pl.when(z > (1 if late else 0))(lambda: down(group, unit, quad, quads).start())
        across(group, unit, quad, quads).start()

    first = 2 * z + 1
    window_copy.wait()
    keep_copy.wait()
    form_filtered(1, 0, lambda piece: swap_in(piece).wait_recv())
    table_copy.wait()

    def along(j, quad, aa, late):
        def copy(send_sem, chip):
            piece = place(first, core, quad, STEP, aa)
            return pltpu.make_async_remote_copy(
                src_ref=stage_ref.at[0, a, pl.ds(quad, STEP)] if aa is a else piece,
                dst_ref=piece,
                send_sem=send_sem.at[first * PARTS + j],
                recv_sem=z_recv.at[first * PARTS + j],
                device_id=at(chip, core),
                device_id_type=MESH,
            )

        pl.when(z < (2 if late else 3))(lambda: copy(up_send, z + 1).start())
        pl.when(z > (1 if late else 0))(lambda: copy(down_send, z - 1).start())

    def ready_first(j, quad, late=False):
        for k in range(3):
            from_source(0, first, j, quad, STEP, k).wait_recv()
            along(j, quad, partners[k], late)
        own(0, first, j, quad, STEP).wait()
        across(first, first * PARTS + j, quad, STEP).start()

    @pl.loop(0, PARTS - 1)
    def _(j):
        form_part(0, j)
        along(j, j * STEP, a, False)
        exchange(0, first, j, j * STEP, STEP)
        pl.when(j > 0)(lambda: ready_first(j - 1, (j - 1) * STEP))

    last = PARTS - 1
    form_part(0, last)
    exchange(0, first, last, KEPT, STEP)
    along(last, KEPT, a, True)
    ready_first(last - 1, KEPT - STEP)

    def ready_last():
        ready_first(last, KEPT, True)

    def whole(action, slot, group, number):
        action(slot, group, number, 0, KEPT)
        action(slot, group, number + 1, KEPT, QUADS - KEPT)

    @pl.when(z == 0)
    def _():
        form_filtered(0, None)
        ready_last()

        @pl.loop(0, PARTS)
        def _(j):
            form_part(2, j)

        whole(exchange, 2, 0, PARTS + 2)

    pl.when(z > 0)(ready_last)

    def take(chip, group):
        upward = ORIGIN[group] < chip
        onward = up if upward else down
        late = late_up if upward else late_down
        end, before = (3, 2) if upward else (0, 1)
        for unit, quad, quads in units_of(group):
            left = late(group, quad)
            if left and chip == end:
                continue
            onward(group, unit, quad, quads).wait_recv()
            if chip != end and not (left and chip == before):
                onward(group, unit, quad, quads).start()
            across(group, unit, quad, quads).start()

    def leave(chip, group):
        number = (UP_LATE if chip == 2 else DOWN_LATE).index(group)
        unit, quad, quads = units_of(group)[-1]
        from_core(group, unit, quad, quads).wait_recv()
        keep_late(number, group).start()

    def in_order(chip, groups, leaving=()):
        @pl.when(z == chip)
        def _():
            for number, group in enumerate(groups):
                take(chip, group)
                for after, done in leaving:
                    if after == number:
                        leave(chip, done)

    in_order(1, [1])
    in_order(2, [3])

    @pl.when(z == 0)
    def _():
        whole(exchanged, 2, 0, PARTS + 2)
        for unit, quad, quads in units_of(0):
            send_own(0, unit, quad, quads)

    second = 2 * z + 2

    @pl.when(z < 3)
    def _():
        halo(core, z).wait_recv()
        form_filtered(2, 1)

        @pl.loop(0, PARTS)
        def _(j):
            form_part(1, j)

        whole(exchange, 1, second, PARTS)

    in_order(1, [0])
    in_order(2, [1])

    @pl.when(z < 3)
    def _():
        whole(exchanged, 1, second, PARTS)
        for j in range(PARTS):
            send_own(second, second * PARTS + j, j * STEP, STEP, late=j == PARTS - 1)

    in_order(0, [3, 4, 5, 6, 7])
    in_order(1, [5, 2, 6, 7], [(0, 3), (1, 4), (1, 5), (3, 6), (3, 7)])
    in_order(2, [7, 0, 4, 2], [(0, 5), (1, 6), (2, 0), (3, 4), (3, 2)])
    in_order(3, [5, 3, 1, 6, 0, 4, 2])

    for piece in range(LANES // SWAP):
        swap_out(piece).wait_send()

    @pl.when((z > 0) & (core == 0))
    def _():
        for which in range(2):
            halo(which, z - 1).wait_send()

    @pl.loop(0, PARTS - 1)
    def _(j):
        exchange_sent(0, first, j, j * STEP, STEP)

    exchange_sent(0, first, last, KEPT, STEP)
    pl.when(z == 0)(lambda: whole(exchange_sent, 2, 0, PARTS + 2))
    pl.when(z < 3)(lambda: whole(exchange_sent, 1, second, PARTS))
    for group in range(GROUPS):
        for unit, quad, quads in units_of(group):
            top = 2 if late_up(group, quad) else 3
            bottom = 1 if late_down(group, quad) else 0
            pl.when((z < top) & (z >= ORIGIN[group]))(
                lambda: up(group, unit, quad, quads).wait_send()
            )
            pl.when((z > bottom) & (z <= ORIGIN[group]))(
                lambda: down(group, unit, quad, quads).wait_send()
            )

            crossed = received = z >= 0
            if late_up(group, quad):
                crossed, received = z < 3, z < 2
            if late_down(group, quad):
                crossed, received = crossed & (z > 0), received & (z > 1)
            pl.when(crossed)(lambda: across(group, unit, quad, quads).wait_send())
            pl.when(received)(lambda: from_core(group, unit, quad, quads).wait_recv())

    for number in range(LATE):
        pl.when(z == 2)(lambda: keep_late(number, UP_LATE[number]).wait())
        pl.when(z == 1)(lambda: keep_late(number, DOWN_LATE[number]).wait())


def gather(voltages, window, table):
    dma = pltpu.SemaphoreType.DMA
    return pl.pallas_call(
        gather_kernel,
        out_shape=[
            jax.ShapeDtypeStruct((GROUPS, 2, 4, KEPT, ROWS, LANES), jnp.bfloat16),
            jax.ShapeDtypeStruct((GROUPS, 2, 4, QUADS - KEPT, ROWS, LANES), jnp.bfloat16),
            jax.ShapeDtypeStruct((LATE, 2, 4, HALF, ROWS, LANES), jnp.bfloat16),
        ],
        in_specs=[
            pl.BlockSpec(memory_space=pltpu.HBM),
            pl.BlockSpec(memory_space=pltpu.HBM),
            pl.BlockSpec(memory_space=pltpu.HBM),
        ],
        out_specs=[pl.BlockSpec(memory_space=pltpu.HBM)] * 3,
        scratch_shapes=[
            pltpu.VMEM((3, LANES, COUNT * FRAME), jnp.bfloat16),
            pltpu.VMEM(window.shape, jnp.float32),
            pltpu.VMEM(table.shape, jnp.bfloat16),
            pltpu.VMEM((COUNT * LANES, FRAME), jnp.bfloat16),
            pltpu.VMEM((3, 4, QUADS, ROWS, LANES), jnp.bfloat16),
            dma((3,)),
            dma((LANES // SWAP,)),
            dma((LANES // SWAP,)),
            dma((2,)),
            dma,
            dma((PARTS + 4,)),
            dma((LATE,)),
            dma((3 * (PARTS + 4),)),
            dma((3 * (PARTS + 4),)),
            dma((UNITS,)),
            dma((UNITS,)),
            dma((UNITS,)),
            dma((UNITS,)),
            dma((UNITS,)),
        ],
        compiler_params=pltpu.CompilerParams(
            collective_id=0, has_side_effects=True, vmem_limit_bytes=62 * 2**20
        ),
        cost_estimate=pl.CostEstimate(
            flops=9 * 2**29, bytes_accessed=2**25, transcendentals=0
        ),
    )(voltages, window, table)


def correlator(ta, spectra_ref, spread_ref, late_ref, columns_ref, left_ref, scale):
    deep, size = columns_ref.shape[:2]
    full = GROUPS * ROWS
    rows = pl.ds(pl.multiple_of(ta * LANES, LANES), LANES)
    channel_of = lax.broadcasted_iota(jnp.int32, (1, size), 1) % 4
    masks = [jnp.where(channel_of == c, 1.0, 0.0).astype(jnp.bfloat16) for c in range(4)]
    columns_ref[:, full:, :] = jnp.zeros((deep, size - full, INPUTS), jnp.bfloat16)

    def prepare(slot, quad, others):
        for group in range(GROUPS):
            down = slice(group * ROWS, (group + 1) * ROWS)
            for aa in range(4):
                for which in range(2):
                    place = (aa * 2 + which) * LANES
                    if group in others:
                        value = late_ref[others.index(group), which, aa, quad]
                    else:
                        value = spectra_ref[group, which, aa, quad]
                    columns_ref[slot, down, place : place + LANES] = value
        left = lax.dot_general(
            columns_ref[slot, :, rows],
            spread_ref[...],
            (((0,), (0,)), ((), ())),
            preferred_element_type=jnp.float32,
        ).astype(jnp.bfloat16)
        for c in range(4):
            for p in range(2):
                place = (c * 2 + p) * LANES
                left_ref[slot, place : place + LANES, :] = (
                    left[:, p * size : (p + 1) * size] * masks[c]
                )

    def multiply(slot, store):
        for block in range(INPUTS // 256):
            here = slice(block * 256, (block + 1) * 256)
            total = jnp.dot(
                left_ref[slot], columns_ref[slot, :, here], preferred_element_type=jnp.float32
            )
            value = (total * scale).astype(jnp.bfloat16)
            for c in range(4):
                for p in range(2):
                    place = (c * 2 + p) * LANES
                    store(p, c, here, value[place : place + LANES])

    return prepare, multiply


def correlate_kernel(where_ref, spectra_ref, spread_ref, out_ref, columns_ref, left_ref, *, scale):
    deep = columns_ref.shape[0]
    prepare, multiply = correlator(
        where_ref[0], spectra_ref, spread_ref, None, columns_ref, left_ref, scale
    )

    @pl.loop(0, spectra_ref.shape[3] // deep)
    def _(step):
        for slot in range(deep):
            prepare(slot, step * deep + slot, ())
        for slot in range(deep):

            def store(p, c, here, value):
                out_ref[p, (step * deep + slot) * 4 + c, :, here] = value

            multiply(slot, store)


def finish_kernel(
    where_ref,
    rest_ref,
    spread_ref,
    late_hbm,
    result_ref,
    out_ref,
    spectra_ref,
    late_ref,
    columns_ref,
    left_ref,
    value_ref,
    load_sem,
    store_sem,
    *,
    scale,
):
    ta, half = where_ref[0], where_ref[1]
    loads = [
        pltpu.make_async_copy(
            rest_ref.at[:, :, :, pl.ds(half * HALF, HALF)], spectra_ref, load_sem.at[0]
        ),
        pltpu.make_async_copy(late_hbm, late_ref, load_sem.at[1]),
    ]
    for load in loads:
        load.start()
    prepare, multiply = correlator(
        ta, spectra_ref, spread_ref, late_ref, columns_ref, left_ref, scale
    )
    for load in loads:
        load.wait()

    def leave(quad):
        channel = (KEPT + half * HALF + quad) * 4
        return pltpu.make_async_copy(
            value_ref.at[quad], out_ref.at[:, pl.ds(channel, 4)], store_sem.at[quad]
        )

    def run(others):
        prepare(0, 0, others)
        for quad in range(HALF):
            if quad + 1 < HALF:
                prepare(quad + 1, quad + 1, others)

            def store(p, c, here, value):
                value_ref[quad, p, c, :, here] = value

            multiply(quad, store)
            leave(quad).start()

    pl.when(ta >= 6)(lambda: run(UP_LATE))
    pl.when(ta < 2)(lambda: run(DOWN_LATE))
    pl.when((ta >= 2) & (ta < 6))(lambda: run(()))
    for quad in range(HALF):
        leave(quad).wait()


def make_spread():
    size = 256
    straight = np.zeros((size, size), np.float32)
    turned = np.zeros((size, size), np.float32)
    for row in range(GROUPS * ROWS):
        straight[row, row] = 1.0
        if row % 8 < 4:
            turned[row + 4, row] = 1.0
        else:
            turned[row - 4, row] = -1.0
    return np.concatenate([straight, turned], axis=1).astype(ml_dtypes.bfloat16)


def correlate(where, spectra, spread, scale):
    quads, deep = spectra.shape[3], 4
    return pl.pallas_call(
        functools.partial(correlate_kernel, scale=scale),
        grid_spec=pltpu.PrefetchScalarGridSpec(
            num_scalar_prefetch=1,
            grid=(quads // deep,),
            in_specs=[
                pl.BlockSpec(
                    (GROUPS, 2, 4, deep, ROWS, LANES), lambda q, where_ref: (0, 0, 0, q, 0, 0)
                ),
                pl.BlockSpec(spread.shape, lambda q, where_ref: (0, 0)),
            ],
            out_specs=pl.BlockSpec(
                (2, 4 * deep, LANES, INPUTS), lambda q, where_ref: (0, q, 0, 0)
            ),
            scratch_shapes=[
                pltpu.VMEM((deep, 256, INPUTS), jnp.bfloat16),
                pltpu.VMEM((deep, 8 * LANES, 256), jnp.bfloat16),
            ],
        ),
        out_shape=jax.ShapeDtypeStruct((2, 4 * QUADS, LANES, INPUTS), jnp.bfloat16),
        compiler_params=pltpu.CompilerParams(vmem_limit_bytes=50 * 2**20),
        cost_estimate=pl.CostEstimate(
            flops=quads * 2**29, bytes_accessed=quads * 5 * 2**19, transcendentals=0
        ),
    )(where, spectra, spread)


def finish_half(where, rest, spread, late, result, scale):
    anywhere = pl.BlockSpec(memory_space=pl.ANY)
    return pl.pallas_call(
        functools.partial(finish_kernel, scale=scale),
        grid_spec=pltpu.PrefetchScalarGridSpec(
            num_scalar_prefetch=1,
            grid=(1,),
            in_specs=[
                anywhere,
                pl.BlockSpec(spread.shape, lambda q, where_ref: (0, 0)),
                anywhere,
                anywhere,
            ],
            out_specs=anywhere,
            scratch_shapes=[
                pltpu.VMEM((GROUPS, 2, 4, HALF, ROWS, LANES), jnp.bfloat16),
                pltpu.VMEM((LATE, 2, 4, HALF, ROWS, LANES), jnp.bfloat16),
                pltpu.VMEM((HALF, 256, INPUTS), jnp.bfloat16),
                pltpu.VMEM((HALF, 8 * LANES, 256), jnp.bfloat16),
                pltpu.VMEM((HALF, 2, 4, LANES, INPUTS), jnp.bfloat16),
                pltpu.SemaphoreType.DMA((2,)),
                pltpu.SemaphoreType.DMA((HALF,)),
            ],
        ),
        out_shape=jax.ShapeDtypeStruct(result.shape, result.dtype),
        input_output_aliases={4: 0},
        compiler_params=pltpu.CompilerParams(vmem_limit_bytes=50 * 2**20),
        cost_estimate=pl.CostEstimate(
            flops=HALF * 2**29, bytes_accessed=HALF * 5 * 2**19, transcendentals=0
        ),
    )(where, rest, spread, late, result)


def shifted(value, axis, steps):
    count = lax.axis_size(axis)
    leading, last = (max(0, -steps), min(count, count - steps))
    return lax.ppermute(value, axis, [(source, source + steps) for source in range(leading, last)])


def plain_window():
    length = TAPS * FRAME
    place = jnp.arange(length, dtype=jnp.float32)
    spread = (place - length / 2 + 0.5) / FRAME
    taper = 0.5 - 0.5 * jnp.cos(2.0 * jnp.pi * (place + 0.5) / length)
    return (jnp.sinc(spread) * taper).reshape(TAPS, FRAME)


def plain_table():
    sample = jnp.arange(FRAME, dtype=jnp.int32)[:, None]
    column = jnp.arange(2 * CHANNELS, dtype=jnp.int32)[None, :]
    channel = column % CHANNELS
    phase = (sample * channel % FRAME).astype(jnp.float32) * (2.0 * jnp.pi / FRAME)
    norm = 1.0 / jnp.sqrt(jnp.float32(FRAME))
    values = jnp.where(column < CHANNELS, jnp.cos(phase), -jnp.sin(phase))
    return (values * norm).astype(jnp.bfloat16)


def left_operand(rows):
    first = jnp.concatenate([rows[0], rows[1]], axis=2)
    second = jnp.concatenate([rows[1], -rows[0]], axis=2)
    return jnp.stack([first, second], axis=0)


def plain_correlate(left, columns):
    return jnp.einsum("pcsi,pcsj->cij", left, columns, preferred_element_type=jnp.float32)


def finish(merged, row_count, scale):
    chan_dev = merged.shape[0]
    shaped = merged.reshape(chan_dev, 2, row_count, merged.shape[2])
    return (jnp.swapaxes(shaped, 0, 1) * scale).astype(jnp.bfloat16)


def plain_per_device(voltages):
    in_dev = voltages.shape[0]
    spec_dev = voltages.shape[1] // FRAME
    n_ta = lax.axis_size("ta")
    frames = voltages.reshape(in_dev, spec_dev, FRAME)
    earlier = shifted(frames, "ta", 1)
    padded = jnp.concatenate([earlier, frames], axis=1)
    window = plain_window()
    filtered = jnp.zeros((in_dev, spec_dev, FRAME), jnp.float32)
    for k in range(TAPS):
        filtered = filtered + window[k] * padded[:, k : k + spec_dev, :].astype(jnp.float32)
    filtered = filtered.astype(jnp.bfloat16)
    table = plain_table()
    spectra = jnp.einsum("isn,nk->ksi", filtered, table, preferred_element_type=jnp.float32).astype(
        jnp.bfloat16
    )
    spectra = spectra.reshape(2, CHANNELS, spec_dev, in_dev)
    row_count = INPUTS // n_ta
    scale = 1.0 / (spec_dev * n_ta)
    own_rows = lax.all_to_all(
        lax.all_to_all(spectra, "aa", split_axis=1, concat_axis=3, tiled=True),
        "ta",
        split_axis=3,
        concat_axis=2,
        tiled=True,
    )
    left = left_operand(own_rows)
    merged = plain_correlate(left, lax.all_gather(own_rows, "ta", axis=3, tiled=True))
    return finish(merged, row_count, scale)


def per_device(voltages):
    in_dev = voltages.shape[0]
    count = voltages.shape[1] // FRAME
    n_ta, n_aa = lax.axis_size("ta"), lax.axis_size("aa")
    fits = in_dev == 2 * LANES and n_ta == 8 and n_aa == 4 and count == COUNT
    if not fits or INPUTS != n_ta * LANES or CHANNELS != 4 * QUADS * n_aa:
        return plain_per_device(voltages)
    scale = 1.0 / (count * n_ta)
    spectra, rest, leaving = gather(
        voltages, jnp.asarray(make_window()), jnp.asarray(make_table())
    )
    ends = [(4, 6), (5, 7), (2, 0), (3, 1)]
    cores = [(6, 7), (7, 6), (0, 1), (1, 0)]
    mine = lax.ppermute(leaving, "ta", ends)
    spread = jnp.asarray(make_spread())
    me = lax.axis_index("ta").astype(jnp.int32)
    core = me % 2
    result = correlate(me.reshape(1), spectra, spread, scale)
    mine, result = lax.optimization_barrier((mine, result))
    others = lax.ppermute(mine, "ta", cores)
    for half, late in ((core, mine), (1 - core, others)):
        result = finish_half(jnp.stack([me, half]), rest, spread, late, result, scale)
    return result


def solution(mesh):
    in_specs = (P("aa", "ta"),)
    out_specs = P(None, "aa", "ta", None)
    return jax.shard_map(
        per_device, mesh=mesh, in_specs=in_specs, out_specs=out_specs, check_vma=False
    )
```

```python
import functools

import jax
import jax.numpy as jnp
import ml_dtypes
import numpy as np
from jax import lax
from jax.experimental import pallas as pl
from jax.experimental.pallas import tpu as pltpu
from jax.sharding import PartitionSpec as P

INPUTS = 1024
FRAME = 2048
CHANNELS = 512
TAPS = 4
LANES = 128
COUNT = 3
QUADS = 32
ROWS = 24
PARTS = 4
STEP = QUADS // PARTS
GROUPS = 8
SWAP = 16
KEPT = QUADS - STEP
HALF = STEP // 2
MESH = pl.DeviceIdType.MESH


def make_window():
    length = TAPS * FRAME
    place = np.arange(length, dtype=np.float64)
    spread = (place - length / 2 + 0.5) / FRAME
    taper = 0.5 - 0.5 * np.cos(2.0 * np.pi * (place + 0.5) / length)
    return (np.sinc(spread) * taper).reshape(TAPS, FRAME).astype(np.float32)


def make_table():
    part, target, quad, real, one = np.meshgrid(
        np.arange(PARTS), np.arange(4), np.arange(QUADS // PARTS), np.arange(2), np.arange(4), indexing="ij"
    )
    channel = (target * QUADS + part * (QUADS // PARTS) + quad) * 4 + one
    channel, real = channel.reshape(-1, 1), real.reshape(-1, 1)
    phase = (channel * np.arange(FRAME)[None, :] % FRAME) * (2.0 * np.pi / FRAME)
    values = np.where(real == 0, np.cos(phase), -np.sin(phase)) / np.sqrt(FRAME)
    return values.astype(ml_dtypes.bfloat16).reshape(PARTS, 2 * CHANNELS // PARTS, FRAME)


ORIGIN = (0, 0, 0, 1, 1, 2, 2, 3)


def units_of(group):
    return [(group * PARTS + j, j * STEP, STEP) for j in range(PARTS)]


UNITS = GROUPS * PARTS

UP_LATE = (5, 6, 2, 4, 0)
DOWN_LATE = (3, 4, 6, 7, 5)
LATE = len(UP_LATE)


def late_up(group, quad):
    return isinstance(quad, int) and quad >= KEPT and group in UP_LATE


def late_down(group, quad):
    return isinstance(quad, int) and quad >= KEPT and group in DOWN_LATE


def gather_kernel(
    voltages_ref,
    window_hbm,
    table_hbm,
    out_ref,
    rest_ref,
    late_ref,
    frames_ref,
    window_ref,
    table_ref,
    filtered_ref,
    stage_ref,
    load_sem,
    swap_send,
    swap_recv,
    halo_send,
    halo_recv,
    own_sem,
    late_sem,
    aa_send,
    aa_recv,
    up_send,
    down_send,
    z_recv,
    core_send,
    core_recv,
):
    a, t = lax.axis_index("aa"), lax.axis_index("ta")
    z, core = t // 2, t % 2
    y, x = a // 2, a % 2
    other = 1 - core

    def at(chip, which, aa=None):
        return {"aa": a if aa is None else aa, "ta": chip * 2 + which}

    partners = [((y + k // 2) % 2) * 2 + (x + k % 2) % 2 for k in range(1, 4)]

    table_copy = pltpu.make_async_copy(table_hbm, table_ref, load_sem.at[0])
    keep_copy = pltpu.make_async_copy(
        voltages_ref.at[pl.ds(core * LANES, LANES)], frames_ref.at[core], load_sem.at[1]
    )
    window_copy = pltpu.make_async_copy(window_hbm, window_ref, load_sem.at[2])

    def swap_piece(piece, which, half):
        rows = pl.ds(pl.multiple_of(piece * SWAP, SWAP), SWAP)
        return pltpu.make_async_remote_copy(
            src_ref=voltages_ref.at[pl.ds(half * LANES + piece * SWAP, SWAP)],
            dst_ref=frames_ref.at[which, rows],
            send_sem=swap_send.at[piece],
            recv_sem=swap_recv.at[piece],
            device_id=at(z, other),
            device_id_type=MESH,
        )

    def swap_out(piece):
        return swap_piece(piece, core, other)

    def swap_in(piece):
        return swap_piece(piece, other, core)

    def halo(which, chip):
        return pltpu.make_async_remote_copy(
            src_ref=voltages_ref.at[pl.ds(which * LANES, LANES)],
            dst_ref=frames_ref.at[2],
            send_sem=halo_send.at[which],
            recv_sem=halo_recv,
            device_id=at(chip, which),
            device_id_type=MESH,
        )

    keep_copy.start()
    window_copy.start()
    table_copy.start()

    barrier = pltpu.get_barrier_semaphore()
    for k in range(3):
        pl.semaphore_signal(barrier, 1, device_id=at(z, core, partners[k]), device_id_type=MESH)
    pl.semaphore_signal(barrier, 1, device_id=at(z, other), device_id_type=MESH)
    for which in range(2):

        @pl.when(z > 0)
        def _():
            pl.semaphore_signal(barrier, 1, device_id=at(z - 1, which), device_id_type=MESH)

        @pl.when(z < 3)
        def _():
            pl.semaphore_signal(barrier, 1, device_id=at(z + 1, which), device_id_type=MESH)

    middle = jnp.where((z > 0) & (z < 3), 2, 0)
    pl.semaphore_wait(barrier, 6 + middle)

    for piece in range(LANES // SWAP):
        swap_out(piece).start()

    @pl.when((z > 0) & (core == 0))
    def _():
        for which in range(2):
            halo(which, z - 1).start()

    def form_filtered(current, earlier, arrived=None):
        def frame(start, place):
            if place < COUNT:
                block, column = earlier, place
            else:
                block, column = current, place - COUNT
            return frames_ref[
                block, pl.ds(start, 16), column * FRAME : (column + 1) * FRAME
            ].astype(jnp.float32)

        @pl.loop(0, LANES // 16)
        def _(step):
            start = pl.multiple_of(step * 16, 16)
            if arrived is not None:
                every = SWAP // 16
                pl.when(step % every == 0)(lambda: arrived(step // every))
            for s in range(COUNT):
                total = None
                for k in range(TAPS):
                    place = s + k + COUNT - TAPS + 1
                    if place < COUNT and earlier is None:
                        continue
                    term = window_ref[k : k + 1, :] * frame(start, place)
                    total = term if total is None else total + term
                filtered_ref[pl.ds(s * LANES + start, 16), :] = total.astype(jnp.bfloat16)

    def form_part(slot, j):
        product = lax.dot_general(
            table_ref[j],
            filtered_ref[...],
            (((1,), (1,)), ((), ())),
            preferred_element_type=jnp.float32,
        )
        pieces = [
            product[:, s * LANES : (s + 1) * LANES].reshape(4 * STEP, 8, LANES)
            for s in range(COUNT)
        ]
        block = jnp.concatenate(pieces, axis=1).astype(jnp.bfloat16)
        stage_ref[slot, :, pl.ds(j * STEP, STEP)] = block.reshape(4, STEP, ROWS, LANES)

    def place(group, which, quad, quads, aa=None):
        ref, start = out_ref, quad
        if isinstance(quad, int) and quad >= KEPT:
            ref, start = rest_ref, quad - KEPT
        if aa is None:
            return ref.at[group, which, :, pl.ds(start, quads)]
        return ref.at[group, which, aa, pl.ds(start, quads)]

    def to_owner(slot, group, number, quad, quads, k):
        return pltpu.make_async_remote_copy(
            src_ref=stage_ref.at[slot, partners[k], pl.ds(quad, quads)],
            dst_ref=place(group, core, quad, quads, a),
            send_sem=aa_send.at[number * 3 + k],
            recv_sem=aa_recv.at[number * 3 + k],
            device_id=at(z, core, partners[k]),
            device_id_type=MESH,
        )

    def from_source(slot, group, number, quad, quads, k):
        return pltpu.make_async_remote_copy(
            src_ref=stage_ref.at[slot, a, pl.ds(quad, quads)],
            dst_ref=place(group, core, quad, quads, partners[k]),
            send_sem=aa_send.at[number * 3 + k],
            recv_sem=aa_recv.at[number * 3 + k],
            device_id=at(z, core, partners[k]),
            device_id_type=MESH,
        )

    def own(slot, group, number, quad, quads):
        return pltpu.make_async_copy(
            stage_ref.at[slot, a, pl.ds(quad, quads)],
            place(group, core, quad, quads, a),
            own_sem.at[number],
        )

    def exchange(slot, group, number, quad, quads):
        own(slot, group, number, quad, quads).start()
        for k in (2, 0, 1):
            to_owner(slot, group, number, quad, quads, k).start()

    def exchanged(slot, group, number, quad, quads):
        own(slot, group, number, quad, quads).wait()
        for k in range(3):
            from_source(slot, group, number, quad, quads, k).wait_recv()

    def exchange_sent(slot, group, number, quad, quads):
        for k in range(3):
            to_owner(slot, group, number, quad, quads, k).wait_send()

    def move(group, unit, quad, quads, which, send_sem, recv_sem, target):
        piece = place(group, which, quad, quads)
        return pltpu.make_async_remote_copy(
            src_ref=piece,
            dst_ref=piece,
            send_sem=send_sem.at[unit],
            recv_sem=recv_sem.at[unit],
            device_id=target,
            device_id_type=MESH,
        )

    def up(group, unit, quad, quads):
        return move(group, unit, quad, quads, core, up_send, z_recv, at(z + 1, core))

    def down(group, unit, quad, quads):
        return move(group, unit, quad, quads, core, down_send, z_recv, at(z - 1, core))

    def across(group, unit, quad, quads):
        return move(group, unit, quad, quads, core, core_send, core_recv, at(z, other))

    def from_core(group, unit, quad, quads):
        return move(group, unit, quad, quads, other, core_send, core_recv, at(z, other))

    def keep_late(number, group):
        return pltpu.make_async_copy(
            rest_ref.at[group, :, :, pl.ds(core * HALF, HALF)],
            late_ref.at[number],
            late_sem.at[number],
        )

    def send_own(group, unit, quad, quads, late=False):
        pl.when(z < (2 if late else 3))(lambda: up(group, unit, quad, quads).start())
        pl.when(z > (1 if late else 0))(lambda: down(group, unit, quad, quads).start())
        across(group, unit, quad, quads).start()

    first = 2 * z + 1
    window_copy.wait()
    keep_copy.wait()
    form_filtered(1, 0, lambda piece: swap_in(piece).wait_recv())
    table_copy.wait()

    def along(j, quad, aa, late):
        def copy(send_sem, chip):
            piece = place(first, core, quad, STEP, aa)
            return pltpu.make_async_remote_copy(
                src_ref=stage_ref.at[0, a, pl.ds(quad, STEP)] if aa is a else piece,
                dst_ref=piece,
                send_sem=send_sem.at[first * PARTS + j],
                recv_sem=z_recv.at[first * PARTS + j],
                device_id=at(chip, core),
                device_id_type=MESH,
            )

        pl.when(z < (2 if late else 3))(lambda: copy(up_send, z + 1).start())
        pl.when(z > (1 if late else 0))(lambda: copy(down_send, z - 1).start())

    def ready_first(j, quad, late=False):
        for k in range(3):
            from_source(0, first, j, quad, STEP, k).wait_recv()
            along(j, quad, partners[k], late)
        own(0, first, j, quad, STEP).wait()
        across(first, first * PARTS + j, quad, STEP).start()

    @pl.loop(0, PARTS - 1)
    def _(j):
        form_part(0, j)
        along(j, j * STEP, a, False)
        exchange(0, first, j, j * STEP, STEP)
        pl.when(j > 0)(lambda: ready_first(j - 1, (j - 1) * STEP))

    last = PARTS - 1
    form_part(0, last)
    exchange(0, first, last, KEPT, STEP)
    along(last, KEPT, a, True)
    ready_first(last - 1, KEPT - STEP)

    def ready_last():
        ready_first(last, KEPT, True)

    def whole(action, slot, group, number):
        action(slot, group, number, 0, KEPT)
        action(slot, group, number + 1, KEPT, QUADS - KEPT)

    @pl.when(z == 0)
    def _():
        form_filtered(0, None)
        ready_last()

        @pl.loop(0, PARTS)
        def _(j):
            form_part(2, j)

        whole(exchange, 2, 0, PARTS + 2)

    pl.when(z > 0)(ready_last)

    def take(chip, group):
        upward = ORIGIN[group] < chip
        onward = up if upward else down
        late = late_up if upward else late_down
        end, before = (3, 2) if upward else (0, 1)
        for unit, quad, quads in units_of(group):
            left = late(group, quad)
            if left and chip == end:
                continue
            onward(group, unit, quad, quads).wait_recv()
            if chip != end and not (left and chip == before):
                onward(group, unit, quad, quads).start()
            across(group, unit, quad, quads).start()

    def leave(chip, group):
        number = (UP_LATE if chip == 2 else DOWN_LATE).index(group)
        unit, quad, quads = units_of(group)[-1]
        from_core(group, unit, quad, quads).wait_recv()
        keep_late(number, group).start()

    def in_order(chip, groups, leaving=()):
        @pl.when(z == chip)
        def _():
            for number, group in enumerate(groups):
                take(chip, group)
                for after, done in leaving:
                    if after == number:
                        leave(chip, done)

    in_order(1, [1])
    in_order(2, [3])

    @pl.when(z == 0)
    def _():
        whole(exchanged, 2, 0, PARTS + 2)
        for unit, quad, quads in units_of(0):
            send_own(0, unit, quad, quads)

    second = 2 * z + 2

    @pl.when(z < 3)
    def _():
        halo(core, z).wait_recv()
        form_filtered(2, 1)

        @pl.loop(0, PARTS)
        def _(j):
            form_part(1, j)

        whole(exchange, 1, second, PARTS)

    in_order(1, [0])
    in_order(2, [1])

    @pl.when(z < 3)
    def _():
        whole(exchanged, 1, second, PARTS)
        for j in range(PARTS):
            send_own(second, second * PARTS + j, j * STEP, STEP, late=j == PARTS - 1)

    in_order(0, [3, 4, 5, 6, 7])
    in_order(1, [5, 2, 6, 7], [(0, 3), (1, 4), (1, 5), (3, 6), (3, 7)])
    in_order(2, [7, 0, 4, 2], [(0, 5), (1, 6), (2, 0), (3, 4), (3, 2)])
    in_order(3, [5, 3, 1, 6, 0, 4, 2])

    for piece in range(LANES // SWAP):
        swap_out(piece).wait_send()

    @pl.when((z > 0) & (core == 0))
    def _():
        for which in range(2):
            halo(which, z - 1).wait_send()

    @pl.loop(0, PARTS - 1)
    def _(j):
        exchange_sent(0, first, j, j * STEP, STEP)

    exchange_sent(0, first, last, KEPT, STEP)
    pl.when(z == 0)(lambda: whole(exchange_sent, 2, 0, PARTS + 2))
    pl.when(z < 3)(lambda: whole(exchange_sent, 1, second, PARTS))
    for group in range(GROUPS):
        for unit, quad, quads in units_of(group):
            top = 2 if late_up(group, quad) else 3
            bottom = 1 if late_down(group, quad) else 0
            pl.when((z < top) & (z >= ORIGIN[group]))(
                lambda: up(group, unit, quad, quads).wait_send()
            )
            pl.when((z > bottom) & (z <= ORIGIN[group]))(
                lambda: down(group, unit, quad, quads).wait_send()
            )

            crossed = received = z >= 0
            if late_up(group, quad):
                crossed, received = z < 3, z < 2
            if late_down(group, quad):
                crossed, received = crossed & (z > 0), received & (z > 1)
            pl.when(crossed)(lambda: across(group, unit, quad, quads).wait_send())
            pl.when(received)(lambda: from_core(group, unit, quad, quads).wait_recv())

    for number in range(LATE):
        pl.when(z == 2)(lambda: keep_late(number, UP_LATE[number]).wait())
        pl.when(z == 1)(lambda: keep_late(number, DOWN_LATE[number]).wait())


def gather(voltages, window, table):
    dma = pltpu.SemaphoreType.DMA
    return pl.pallas_call(
        gather_kernel,
        out_shape=[
            jax.ShapeDtypeStruct((GROUPS, 2, 4, KEPT, ROWS, LANES), jnp.bfloat16),
            jax.ShapeDtypeStruct((GROUPS, 2, 4, QUADS - KEPT, ROWS, LANES), jnp.bfloat16),
            jax.ShapeDtypeStruct((LATE, 2, 4, HALF, ROWS, LANES), jnp.bfloat16),
        ],
        in_specs=[
            pl.BlockSpec(memory_space=pltpu.HBM),
            pl.BlockSpec(memory_space=pltpu.HBM),
            pl.BlockSpec(memory_space=pltpu.HBM),
        ],
        out_specs=[pl.BlockSpec(memory_space=pltpu.HBM)] * 3,
        scratch_shapes=[
            pltpu.VMEM((3, LANES, COUNT * FRAME), jnp.bfloat16),
            pltpu.VMEM(window.shape, jnp.float32),
            pltpu.VMEM(table.shape, jnp.bfloat16),
            pltpu.VMEM((COUNT * LANES, FRAME), jnp.bfloat16),
            pltpu.VMEM((3, 4, QUADS, ROWS, LANES), jnp.bfloat16),
            dma((3,)),
            dma((LANES // SWAP,)),
            dma((LANES // SWAP,)),
            dma((2,)),
            dma,
            dma((PARTS + 4,)),
            dma((LATE,)),
            dma((3 * (PARTS + 4),)),
            dma((3 * (PARTS + 4),)),
            dma((UNITS,)),
            dma((UNITS,)),
            dma((UNITS,)),
            dma((UNITS,)),
            dma((UNITS,)),
        ],
        compiler_params=pltpu.CompilerParams(
            collective_id=0, has_side_effects=True, vmem_limit_bytes=62 * 2**20
        ),
        cost_estimate=pl.CostEstimate(
            flops=9 * 2**29, bytes_accessed=2**25, transcendentals=0
        ),
    )(voltages, window, table)


def correlator(ta, spectra_ref, spread_ref, late_ref, columns_ref, left_ref, scale):
    deep, size = columns_ref.shape[:2]
    full = GROUPS * ROWS
    rows = pl.ds(pl.multiple_of(ta * LANES, LANES), LANES)
    channel_of = lax.broadcasted_iota(jnp.int32, (1, size), 1) % 4
    masks = [jnp.where(channel_of == c, 1.0, 0.0).astype(jnp.bfloat16) for c in range(4)]
    columns_ref[:, full:, :] = jnp.zeros((deep, size - full, INPUTS), jnp.bfloat16)

    def fill(slot, quad, others):
        for group in range(GROUPS):
            down = slice(group * ROWS, (group + 1) * ROWS)
            for aa in range(4):
                for which in range(2):
                    place = (aa * 2 + which) * LANES
                    if group in others:
                        value = late_ref[others.index(group), which, aa, quad]
                    else:
                        value = spectra_ref[group, which, aa, quad]
                    columns_ref[slot, down, place : place + LANES] = value

    def turn(slots):
        own = jnp.concatenate([columns_ref[slot, :, rows] for slot in slots], axis=1)
        left = lax.dot_general(
            own,
            spread_ref[...],
            (((0,), (0,)), ((), ())),
            preferred_element_type=jnp.float32,
        ).astype(jnp.bfloat16)
        for number, slot in enumerate(slots):
            here = slice(number * LANES, (number + 1) * LANES)
            for c in range(4):
                for p in range(2):
                    place = (c * 2 + p) * LANES
                    left_ref[slot, place : place + LANES, :] = (
                        left[here, p * size : (p + 1) * size] * masks[c]
                    )

    def prepare(slot, quad, others):
        fill(slot, quad, others)
        turn([slot])

    def multiply(slot, store):
        for block in range(INPUTS // 256):
            here = slice(block * 256, (block + 1) * 256)
            total = jnp.dot(
                left_ref[slot], columns_ref[slot, :, here], preferred_element_type=jnp.float32
            )
            value = (total * scale).astype(jnp.bfloat16)
            for c in range(4):
                for p in range(2):
                    place = (c * 2 + p) * LANES
                    store(p, c, here, value[place : place + LANES])

    return fill, turn, prepare, multiply


def correlate_kernel(where_ref, spectra_ref, spread_ref, out_ref, columns_ref, left_ref, *, scale):
    deep = columns_ref.shape[0]
    fill, turn, _, multiply = correlator(
        where_ref[0], spectra_ref, spread_ref, None, columns_ref, left_ref, scale
    )

    @pl.loop(0, spectra_ref.shape[3] // deep)
    def _(step):
        for slot in range(deep):
            fill(slot, step * deep + slot, ())
        turn(range(deep))
        for slot in range(deep):

            def store(p, c, here, value):
                out_ref[p, (step * deep + slot) * 4 + c, :, here] = value

            multiply(slot, store)


def finish_kernel(
    where_ref,
    rest_ref,
    spread_ref,
    late_hbm,
    result_ref,
    out_ref,
    spectra_ref,
    late_ref,
    columns_ref,
    left_ref,
    value_ref,
    load_sem,
    store_sem,
    *,
    scale,
):
    ta, half = where_ref[0], where_ref[1]
    loads = [
        pltpu.make_async_copy(
            rest_ref.at[:, :, :, pl.ds(half * HALF, HALF)], spectra_ref, load_sem.at[0]
        ),
        pltpu.make_async_copy(late_hbm, late_ref, load_sem.at[1]),
    ]
    for load in loads:
        load.start()
    _, _, prepare, multiply = correlator(
        ta, spectra_ref, spread_ref, late_ref, columns_ref, left_ref, scale
    )
    for load in loads:
        load.wait()

    def leave(quad):
        channel = (KEPT + half * HALF + quad) * 4
        return pltpu.make_async_copy(
            value_ref.at[quad], out_ref.at[:, pl.ds(channel, 4)], store_sem.at[quad]
        )

    def run(others):
        prepare(0, 0, others)
        for quad in range(HALF):
            if quad + 1 < HALF:
                prepare(quad + 1, quad + 1, others)

            def store(p, c, here, value):
                value_ref[quad, p, c, :, here] = value

            multiply(quad, store)
            leave(quad).start()

    pl.when(ta >= 6)(lambda: run(UP_LATE))
    pl.when(ta < 2)(lambda: run(DOWN_LATE))
    pl.when((ta >= 2) & (ta < 6))(lambda: run(()))
    for quad in range(HALF):
        leave(quad).wait()


def make_spread():
    size = 256
    straight = np.zeros((size, size), np.float32)
    turned = np.zeros((size, size), np.float32)
    for row in range(GROUPS * ROWS):
        straight[row, row] = 1.0
        if row % 8 < 4:
            turned[row + 4, row] = 1.0
        else:
            turned[row - 4, row] = -1.0
    return np.concatenate([straight, turned], axis=1).astype(ml_dtypes.bfloat16)


def correlate(where, spectra, spread, scale):
    quads, deep = spectra.shape[3], 4
    return pl.pallas_call(
        functools.partial(correlate_kernel, scale=scale),
        grid_spec=pltpu.PrefetchScalarGridSpec(
            num_scalar_prefetch=1,
            grid=(quads // deep,),
            in_specs=[
                pl.BlockSpec(
                    (GROUPS, 2, 4, deep, ROWS, LANES), lambda q, where_ref: (0, 0, 0, q, 0, 0)
                ),
                pl.BlockSpec(spread.shape, lambda q, where_ref: (0, 0)),
            ],
            out_specs=pl.BlockSpec(
                (2, 4 * deep, LANES, INPUTS), lambda q, where_ref: (0, q, 0, 0)
            ),
            scratch_shapes=[
                pltpu.VMEM((deep, 256, INPUTS), jnp.bfloat16),
                pltpu.VMEM((deep, 8 * LANES, 256), jnp.bfloat16),
            ],
        ),
        out_shape=jax.ShapeDtypeStruct((2, 4 * QUADS, LANES, INPUTS), jnp.bfloat16),
        compiler_params=pltpu.CompilerParams(vmem_limit_bytes=50 * 2**20),
        cost_estimate=pl.CostEstimate(
            flops=quads * 2**29, bytes_accessed=quads * 5 * 2**19, transcendentals=0
        ),
    )(where, spectra, spread)


def finish_half(where, rest, spread, late, result, scale):
    anywhere = pl.BlockSpec(memory_space=pl.ANY)
    return pl.pallas_call(
        functools.partial(finish_kernel, scale=scale),
        grid_spec=pltpu.PrefetchScalarGridSpec(
            num_scalar_prefetch=1,
            grid=(1,),
            in_specs=[
                anywhere,
                pl.BlockSpec(spread.shape, lambda q, where_ref: (0, 0)),
                anywhere,
                anywhere,
            ],
            out_specs=anywhere,
            scratch_shapes=[
                pltpu.VMEM((GROUPS, 2, 4, HALF, ROWS, LANES), jnp.bfloat16),
                pltpu.VMEM((LATE, 2, 4, HALF, ROWS, LANES), jnp.bfloat16),
                pltpu.VMEM((HALF, 256, INPUTS), jnp.bfloat16),
                pltpu.VMEM((HALF, 8 * LANES, 256), jnp.bfloat16),
                pltpu.VMEM((HALF, 2, 4, LANES, INPUTS), jnp.bfloat16),
                pltpu.SemaphoreType.DMA((2,)),
                pltpu.SemaphoreType.DMA((HALF,)),
            ],
        ),
        out_shape=jax.ShapeDtypeStruct(result.shape, result.dtype),
        input_output_aliases={4: 0},
        compiler_params=pltpu.CompilerParams(vmem_limit_bytes=50 * 2**20),
        cost_estimate=pl.CostEstimate(
            flops=HALF * 2**29, bytes_accessed=HALF * 5 * 2**19, transcendentals=0
        ),
    )(where, rest, spread, late, result)


def shifted(value, axis, steps):
    count = lax.axis_size(axis)
    leading, last = (max(0, -steps), min(count, count - steps))
    return lax.ppermute(value, axis, [(source, source + steps) for source in range(leading, last)])


def plain_window():
    length = TAPS * FRAME
    place = jnp.arange(length, dtype=jnp.float32)
    spread = (place - length / 2 + 0.5) / FRAME
    taper = 0.5 - 0.5 * jnp.cos(2.0 * jnp.pi * (place + 0.5) / length)
    return (jnp.sinc(spread) * taper).reshape(TAPS, FRAME)


def plain_table():
    sample = jnp.arange(FRAME, dtype=jnp.int32)[:, None]
    column = jnp.arange(2 * CHANNELS, dtype=jnp.int32)[None, :]
    channel = column % CHANNELS
    phase = (sample * channel % FRAME).astype(jnp.float32) * (2.0 * jnp.pi / FRAME)
    norm = 1.0 / jnp.sqrt(jnp.float32(FRAME))
    values = jnp.where(column < CHANNELS, jnp.cos(phase), -jnp.sin(phase))
    return (values * norm).astype(jnp.bfloat16)


def left_operand(rows):
    first = jnp.concatenate([rows[0], rows[1]], axis=2)
    second = jnp.concatenate([rows[1], -rows[0]], axis=2)
    return jnp.stack([first, second], axis=0)


def plain_correlate(left, columns):
    return jnp.einsum("pcsi,pcsj->cij", left, columns, preferred_element_type=jnp.float32)


def finish(merged, row_count, scale):
    chan_dev = merged.shape[0]
    shaped = merged.reshape(chan_dev, 2, row_count, merged.shape[2])
    return (jnp.swapaxes(shaped, 0, 1) * scale).astype(jnp.bfloat16)


def plain_per_device(voltages):
    in_dev = voltages.shape[0]
    spec_dev = voltages.shape[1] // FRAME
    n_ta = lax.axis_size("ta")
    frames = voltages.reshape(in_dev, spec_dev, FRAME)
    earlier = shifted(frames, "ta", 1)
    padded = jnp.concatenate([earlier, frames], axis=1)
    window = plain_window()
    filtered = jnp.zeros((in_dev, spec_dev, FRAME), jnp.float32)
    for k in range(TAPS):
        filtered = filtered + window[k] * padded[:, k : k + spec_dev, :].astype(jnp.float32)
    filtered = filtered.astype(jnp.bfloat16)
    table = plain_table()
    spectra = jnp.einsum("isn,nk->ksi", filtered, table, preferred_element_type=jnp.float32).astype(
        jnp.bfloat16
    )
    spectra = spectra.reshape(2, CHANNELS, spec_dev, in_dev)
    row_count = INPUTS // n_ta
    scale = 1.0 / (spec_dev * n_ta)
    own_rows = lax.all_to_all(
        lax.all_to_all(spectra, "aa", split_axis=1, concat_axis=3, tiled=True),
        "ta",
        split_axis=3,
        concat_axis=2,
        tiled=True,
    )
    left = left_operand(own_rows)
    merged = plain_correlate(left, lax.all_gather(own_rows, "ta", axis=3, tiled=True))
    return finish(merged, row_count, scale)


def per_device(voltages):
    in_dev = voltages.shape[0]
    count = voltages.shape[1] // FRAME
    n_ta, n_aa = lax.axis_size("ta"), lax.axis_size("aa")
    fits = in_dev == 2 * LANES and n_ta == 8 and n_aa == 4 and count == COUNT
    if not fits or INPUTS != n_ta * LANES or CHANNELS != 4 * QUADS * n_aa:
        return plain_per_device(voltages)
    scale = 1.0 / (count * n_ta)
    spectra, rest, leaving = gather(
        voltages, jnp.asarray(make_window()), jnp.asarray(make_table())
    )
    ends = [(4, 6), (5, 7), (2, 0), (3, 1)]
    cores = [(6, 7), (7, 6), (0, 1), (1, 0)]
    mine = lax.ppermute(leaving, "ta", ends)
    spread = jnp.asarray(make_spread())
    me = lax.axis_index("ta").astype(jnp.int32)
    core = me % 2
    result = correlate(me.reshape(1), spectra, spread, scale)
    mine, result = lax.optimization_barrier((mine, result))
    others = lax.ppermute(mine, "ta", cores)
    for half, late in ((core, mine), (1 - core, others)):
        result = finish_half(jnp.stack([me, half]), rest, spread, late, result, scale)
    return result


def solution(mesh):
    in_specs = (P("aa", "ta"),)
    out_specs = P(None, "aa", "ta", None)
    return jax.shard_map(
        per_device, mesh=mesh, in_specs=in_specs, out_specs=out_specs, check_vma=False
    )
```
